128 devices in a mesh: patch: 16 (over y, x), col: 8 (over z, core).
Axes of the slice: x: 4, y: 4, z: 4, core: 2. Of those that a mesh axis runs over, the one named last changes fastest.
Arguments:
- potential0: float32 [512, 16, 128], P(('patch', 'col')), may hold values from -3 to 3
- source_term: float32 [512, 16, 128], P(('patch', 'col')), may hold values from -9 to 9
- self_coef: float32 [512, 128], P(('patch', 'col')), may hold values from 1 to 4
- nearfield: float32 [512, 24, 128, 128], P(('patch', 'col')), may hold values from -0.109375 to 0.109375
- precond: float32 [512, 128, 128], P(('patch', 'col')), may hold values from -1 to 2
- exch_current: float32 [512, 128], P(('patch', 'col')), may hold values from 0.05 to 0.5
- conductance: float32 [512, 128], P(('patch', 'col')), may hold values from 0.1 to 1
- member: int32 [512, 128], P(('patch', 'col')), may hold values from 0 to 63
- anode_drive: float32 [64], replicated, may hold values from -1 to 1
- pair_source: int32 [512, 24], P(('patch', 'col')), may hold values from 0 to 39
- pair_count: int32 [512], P(('patch', 'col')), may hold values from 1 to 24, as said below
Outputs:
- potential: float32 [512, 16, 128], P(('patch', 'col'))
- residual: float32 [512, 16, 128], P(('patch', 'col'))
The draws below stay inside these ranges and needn't reach their ends.
Inputs may be any that keep to these rules, and one draw needn't show every extreme that they name: Slots k < pair_count[b] of block b are live; some block has all 24 slots live, and the blocks of some devices hold far more live pairs than those of others.
All inputs are finite; a program needn't handle non-finite values.
Results may differ from the reference program's by a relative error of at most 0.0003.
Values sent between devices are 32-bit elements; how exact they have to be, the bound alone decides.
A program may use at most 64 MiB of HBM per device.

```python
import math
import jax
import jax.numpy as jnp
from jax import lax

B = 128
COLS = 16
K = 24
MEMBERS = 64
NEWTON = 2
GMRES = 2
NB_DEV = 4
PATCHES = 16
PATCH_BLOCKS = 32
BLOCKS = 512
SLOTS = 40


def draw_source_term(key, part):
    first, second = jax.random.split(key, 2)
    base = jnp.clip(jax.random.normal(first, (BLOCKS, COLS, B), jnp.float32), -3.0, 3.0)
    panel_scale = jnp.exp(jax.random.uniform(second, (BLOCKS, 1, B), jnp.float32) * math.log(10.0))
    rising = jnp.exp(math.log(3.0) * jnp.arange(BLOCKS, dtype=jnp.float32) / BLOCKS)[:, None, None]
    return 0.1 * base * panel_scale * rising


def draw_precond(key, part):
    first, second = jax.random.split(key, 2)
    scales = 0.3 * jnp.exp(jax.random.uniform(first, (BLOCKS, B, 1), jnp.float32) * math.log(1.0 / 0.3))
    identity = (jnp.arange(B)[:, None] == jnp.arange(B)[None, :]).astype(jnp.float32)
    spread = jnp.clip(jax.random.normal(second, (BLOCKS, B, B), jnp.float32), -4.0, 4.0) * (0.3 / math.sqrt(B))
    return scales * identity[None] + spread


def draw_pair_count(key, part):
    first, second, third, fourth = jax.random.split(key, 4)
    devices = BLOCKS // NB_DEV
    heavy = jax.random.randint(first, (devices,), 0, 4) == 0
    chosen = jax.random.randint(second, (), 0, devices)
    heavy = heavy | (jnp.arange(devices) == chosen)
    heavy_block = jnp.repeat(heavy, NB_DEV)
    light_load = jax.random.randint(third, (BLOCKS,), max(K // 4, 1), K // 2 + 1)
    full_load = K - jax.random.randint(fourth, (BLOCKS,), 0, max(K // 4, 1))
    counts = jnp.where(heavy_block, full_load, light_load)
    return counts.at[0].set(K).astype(jnp.int32)


def set_ends(drawn, stream_key, smallest, top_value):
    shape = drawn.shape
    spot = [jax.random.randint(jax.random.fold_in(stream_key, axis), (), 0, shape[axis]) for axis in range(len(shape))]
    drawn = drawn.at[tuple(spot)].set(smallest)
    longest = shape.index(max(shape))
    spot[longest] = (spot[longest] + 1) % shape[longest]
    return drawn.at[tuple(spot)].set(top_value)


def shard_levels(stream_key, extent, pieces, smallest, largest):
    loudness, own = 1.0, jax.random.fold_in(stream_key, 6)
    for position, shards_of in pieces:
        draws = jnp.exp(jax.random.uniform(jax.random.fold_in(own, position), (shards_of,), jnp.float32, smallest / len(pieces), largest / len(pieces)))
        loudness = loudness * jnp.repeat(draws, extent[position] // shards_of).reshape([-1 if axis == position else 1 for axis in range(len(extent))])
    return loudness


def centred(own_key, extent, deviation, most, pieces=(), kind=jnp.bfloat16):
    gain = shard_levels(own_key, extent, pieces, -0.22, 0.18) if pieces else 1.0
    drawn = jax.random.normal(own_key, extent, jnp.float32) * deviation * gain
    return jnp.minimum(jnp.maximum(drawn, -most), most).astype(kind)


def setup_inputs(seed: int = 0) -> dict:
    splits = jax.random.split(jax.random.key(seed), 12)
    potential0 = centred(splits[0], (BLOCKS, COLS, B), 0.5, 3.0, ((0, 128),), jnp.float32)
    source_term = draw_source_term(jax.random.fold_in(splits[11], 71), 0)
    self_coef = jnp.clip(jnp.exp(math.log(4.0) - 1.3862944 * jax.random.uniform(splits[2], (BLOCKS, B), jnp.float32) ** shard_levels(splits[2], (BLOCKS, B), ((0, 128),), -0.2, 0.2)), 1.0, 4.0)
    nearfield = centred(splits[3], (BLOCKS, K, B, B), (K * B) ** -0.5, 0.109375, ((0, 128),), jnp.float32)
    precond = draw_precond(jax.random.fold_in(splits[11], 71), 0)
    exch_current = jnp.clip(jnp.exp(math.log(0.5) - 2.3025851 * jax.random.uniform(splits[5], (BLOCKS, B), jnp.float32) ** shard_levels(splits[5], (BLOCKS, B), ((0, 128),), -0.2, 0.2)), 0.05, 0.5)
    conductance = jnp.clip(jnp.exp(math.log(1.0) - 2.3025851 * jax.random.uniform(splits[6], (BLOCKS, B), jnp.float32) ** shard_levels(splits[6], (BLOCKS, B), ((0, 128),), -0.2, 0.2)), 0.1, 1.0)
    member = set_ends(jax.random.randint(splits[7], (BLOCKS, B), 0, MEMBERS), jax.random.fold_in(splits[7], 1), 0, MEMBERS - 1).astype(jnp.int32)
    anode_drive = jnp.clip(jax.random.uniform(splits[8], (MEMBERS,), jnp.float32, -1.0, 1.0), -1.0, 1.0)
    pair_source = set_ends(jax.random.randint(splits[9], (BLOCKS, K), 0, SLOTS), jax.random.fold_in(splits[9], 1), 0, SLOTS - 1).astype(jnp.int32)
    pair_count = draw_pair_count(jax.random.fold_in(splits[11], 71), 0)
    return dict(potential0=potential0, source_term=source_term, self_coef=self_coef, nearfield=nearfield, precond=precond, exch_current=exch_current, conductance=conductance, member=member, anode_drive=anode_drive, pair_source=pair_source, pair_count=pair_count)


ALPHA = 0.6
BETA = 0.4
EPS = 1e-06

def source_index(pair_source):
    blocks = jnp.arange(BLOCKS, dtype=jnp.int32)
    patch = blocks // PATCH_BLOCKS
    group = blocks % PATCH_BLOCKS // NB_DEV
    own_block = patch[:, None] * PATCH_BLOCKS + pair_source
    earlier = ((patch - 1) % PATCHES * PATCH_BLOCKS + group * NB_DEV)[:, None] + (pair_source - PATCH_BLOCKS)
    later = ((patch + 1) % PATCHES * PATCH_BLOCKS + group * NB_DEV)[:, None] + (pair_source - PATCH_BLOCKS - NB_DEV)
    chosen = jnp.where(pair_source < PATCH_BLOCKS, own_block, jnp.where(pair_source < PATCH_BLOCKS + NB_DEV, earlier, later))
    return chosen.astype(jnp.int32)

def near_field(field, nearfield, index, live_mask):
    devices = BLOCKS // NB_DEV

    def one_device(inputs):
        matrices, rows, mask = inputs
        sources = field[rows] * mask[:, :, None, None]
        return jnp.einsum('bkij,bkcj->bci', matrices, sources, precision=lax.Precision.HIGHEST)
    result = lax.map(one_device, (nearfield.reshape(devices, NB_DEV, K, B, B), index.reshape(devices, NB_DEV, K), live_mask.reshape(devices, NB_DEV, K)))
    return result.reshape(BLOCKS, COLS, B)

def least_squares(columns, beta):
    depth = len(columns)
    hessen = jnp.zeros((beta.shape[0], depth + 1, depth), jnp.float32)
    for place in range(depth):
        hessen = hessen.at[:, :place + 2, place].set(columns[place].T)
    gram = jnp.einsum('cij,cik->cjk', hessen, hessen, precision=lax.Precision.HIGHEST)
    right = beta[:, None] * hessen[:, 0, :]
    lower = jnp.linalg.cholesky(gram)
    middle = jax.scipy.linalg.solve_triangular(lower, right[:, :, None], lower=True)
    return jax.scipy.linalg.solve_triangular(lower, middle, lower=True, trans=1)[:, :, 0]

def reference(potential0, source_term, self_coef, nearfield, precond, exch_current, conductance, member, anode_drive, pair_source, pair_count):
    index = source_index(pair_source)
    live_mask = (jnp.arange(K, dtype=jnp.int32)[None, :] < pair_count[:, None]).astype(jnp.float32)
    member_drive = anode_drive[member]
    diagonal = self_coef[:, None, :]
    current = exch_current[:, None, :]
    conduct = conductance[:, None, :]

    def column_sum(left, right):
        return lax.optimization_barrier(jnp.sum(left * right, axis=(0, 2)))

    def mismatch(field):
        grow = jnp.exp(ALPHA * field)
        shrink = jnp.exp(-BETA * field)
        value = diagonal * field + near_field(field, nearfield, index, live_mask) + current * (grow - shrink) + conduct * (field - member_drive[:, None, :]) - source_term
        slope = current * (ALPHA * grow + BETA * shrink) + conduct
        return (value, slope)
    field = potential0
    for newton in range(NEWTON):
        value, slope = mismatch(field)
        start = -value
        beta = jnp.sqrt(column_sum(start, start) + EPS)
        basis = [start / beta[None, :, None]]
        directions = []
        columns = []
        for step in range(GMRES):
            direction = jnp.einsum('bij,bcj->bci', precond, basis[step], precision=lax.Precision.HIGHEST)
            directions.append(direction)
            image = diagonal * direction + near_field(direction, nearfield, index, live_mask) + slope * direction
            coeffs = []
            for place in range(step + 1):
                coeff = column_sum(basis[place], image)
                image = image - coeff[None, :, None] * basis[place]
                coeffs.append(coeff)
            norm = jnp.sqrt(column_sum(image, image) + EPS)
            basis.append(image / norm[None, :, None])
            columns.append(jnp.stack(coeffs + [norm]))
        weights = least_squares(columns, beta)
        update = jnp.zeros_like(field)
        for step in range(GMRES):
            update = update + weights[:, step][None, :, None] * directions[step]
        field = field + update
    final_value, final_slope = mismatch(field)
    return (field, final_value)
```

```python
import functools

import jax
import jax.numpy as jnp
from jax import lax
from jax.experimental import pallas as pl
from jax.experimental.pallas import tpu as pltpu
from jax.sharding import PartitionSpec as P

NEWTON = 2

ALPHA = 0.6
BETA = 0.4
EPS = 1e-06

MESH = pl.DeviceIdType.MESH
F32 = jnp.float32
BF16 = jnp.bfloat16


def halves(array):
    high = array.astype(BF16)
    low = (array - high.astype(F32)).astype(BF16)
    return high, low


def both_halves(left, right):
    rows = left.shape[0] // 2
    wide = lax.dot_general(left, right, (((1,), (1,)), ((), ())), preferred_element_type=F32)
    half = wide.shape[1] // 2
    return wide[:rows, :half] + (wide[rows:, :half] + wide[:rows, half:]) + wide[rows:, half:]


def kernel(
    patches,
    cols,
    drive_s,
    source_s,
    count_s,
    potential0_h,
    source_term_h,
    self_coef_h,
    nearfield_h,
    precond_h,
    current_h,
    conduct_h,
    member_h,
    potential_o,
    residual_o,
    potential0,
    source_term,
    panels,
    member,
    staged,
    weights,
    precond_f,
    precond_w,
    exchange,
    split,
    near_out,
    sums_a,
    sums_b,
    load_sem,
    send_sem,
    recv_sem,
    sum_send,
    sum_recv,
):
    patch = lax.axis_index("patch")
    col = lax.axis_index("col")
    blocks, pairs = source_s.shape
    columns = potential0.shape[1]
    slots = exchange.shape[1]

    loads = [
        pltpu.make_async_copy(potential0_h, potential0, load_sem.at[0]),
        pltpu.make_async_copy(source_term_h, source_term, load_sem.at[1]),
        pltpu.make_async_copy(self_coef_h, panels.at[0], load_sem.at[2]),
        pltpu.make_async_copy(current_h, panels.at[1], load_sem.at[3]),
        pltpu.make_async_copy(conduct_h, panels.at[2], load_sem.at[4]),
        pltpu.make_async_copy(member_h, member, load_sem.at[5]),
        pltpu.make_async_copy(precond_h, precond_f, load_sem.at[6]),
    ]
    matrix_loads = [
        pltpu.make_async_copy(nearfield_h.at[b], staged.at[b], load_sem.at[7 + b])
        for b in range(blocks)
    ]
    for load in loads + matrix_loads:
        load.start()

    def peer_col(step):
        return lax.rem(col + step, cols)

    def peer_patch(step):
        return lax.rem(patch + step, patches)

    barrier = pltpu.get_barrier_semaphore()
    for step in range(1, cols):
        pl.semaphore_signal(
            barrier, inc=1, device_id={"col": peer_col(step)}, device_id_type=MESH
        )
    for step in range(1, patches):
        pl.semaphore_signal(
            barrier, inc=1, device_id={"patch": peer_patch(step)}, device_id_type=MESH
        )
    pl.semaphore_wait(barrier, cols + patches - 2)

    own = pl.ds(pl.multiple_of(col * blocks, blocks), blocks)
    before = pl.ds(cols * blocks, blocks)
    after = pl.ds((cols + 1) * blocks, blocks)
    incoming = pl.ds(0, slots - blocks)

    def start_exchange(turn, value):
        exchange[turn, own] = value
        mine = exchange.at[turn, own]

        def send(place, target):
            pltpu.make_async_remote_copy(
                src_ref=mine,
                dst_ref=exchange.at[turn, place],
                send_sem=send_sem.at[turn],
                recv_sem=recv_sem.at[turn],
                device_id=target,
                device_id_type=MESH,
            ).start()

        for step in range(1, cols):
            send(own, {"col": peer_col(step)})
        send(before, {"patch": peer_patch(1)})
        send(after, {"patch": peer_patch(patches - 1)})

    def exchange_copy(turn):
        return pltpu.make_async_remote_copy(
            src_ref=exchange.at[turn, incoming],
            dst_ref=exchange.at[turn, incoming],
            send_sem=send_sem.at[turn],
            recv_sem=recv_sem.at[turn],
            device_id={"col": peer_col(1)},
            device_id_type=MESH,
        )

    def near_field(turn):
        exchange_copy(turn).wait_recv()
        high, low = halves(exchange[turn])
        split[:, :columns] = high
        split[:, columns:] = low

        def block(b, carry):
            left = jnp.concatenate([split[source_s[b, k]] for k in range(pairs)], axis=1)
            near_out[b] = both_halves(left, weights[b])
            return carry

        lax.fori_loop(0, blocks, block, 0)
        return near_out[...]

    def start_sums_a(turn, parts):
        lane = lax.broadcasted_iota(jnp.int32, (columns, 128), 1)
        packed = jnp.zeros((columns, 128), F32)
        for place, (left, right) in enumerate(parts):
            value = jnp.sum(jnp.sum(left * right, axis=0), axis=1, keepdims=True)
            packed = jnp.where(lane == place, value, packed)
        sums_a[turn, patch] = packed
        for step in range(1, patches):
            pltpu.make_async_remote_copy(
                src_ref=sums_a.at[turn, patch],
                dst_ref=sums_a.at[turn, patch],
                send_sem=sum_send.at[0, turn],
                recv_sem=sum_recv.at[0, turn],
                device_id={"patch": peer_patch(step)},
                device_id_type=MESH,
            ).start()

    def sums_copy(stage, turn):
        buffer, size = ((sums_a, patches), (sums_b, cols))[stage]
        return pltpu.make_async_remote_copy(
            src_ref=buffer.at[turn, pl.ds(0, size - 1)],
            dst_ref=buffer.at[turn, pl.ds(0, size - 1)],
            send_sem=sum_send.at[stage, turn],
            recv_sem=sum_recv.at[stage, turn],
            device_id={"col": peer_col(1)},
            device_id_type=MESH,
        )

    def start_sums_b(turn):
        sums_copy(0, turn).wait_recv()
        sums_b[turn, col] = jnp.sum(sums_a[turn], axis=0)
        for step in range(1, cols):
            pltpu.make_async_remote_copy(
                src_ref=sums_b.at[turn, col],
                dst_ref=sums_b.at[turn, col],
                send_sem=sum_send.at[1, turn],
                recv_sem=sum_recv.at[1, turn],
                device_id={"col": peer_col(step)},
                device_id_type=MESH,
            ).start()

    def finish_sums(turn, count):
        sums_copy(1, turn).wait_recv()
        total = jnp.sum(sums_b[turn], axis=0)
        return [
            jnp.broadcast_to(total[:, place : place + 1], (columns, 128))
            for place in range(count)
        ]

    for load in loads:
        load.wait()
    start_exchange(0, potential0[...])

    owner = member[...]
    drive = jnp.zeros(owner.shape, F32)
    for place in range(drive_s.shape[0]):
        drive = jnp.where(owner == place, drive_s[place], drive)
    panels[3] = drive
    high, low = halves(precond_f[...])
    precond_w[:, :128] = high
    precond_w[:, 128:] = low

    for b in range(blocks):
        matrix_loads[b].wait()

        def prepare(k, carry, b=b):
            live = jnp.where(k < count_s[b], 1.0, 0.0).astype(F32)
            high, low = halves(staged[b, k] * live)
            place = pl.ds(pl.multiple_of(k * 128, 128), 128)
            weights[b, :128, place] = high
            weights[b, 128:, place] = low
            return carry

        lax.fori_loop(0, pairs, prepare, 0, unroll=4)

    def panel(place):
        return panels[place][:, None, :]

    def mismatch(field, near_value):
        grow = jnp.exp(ALPHA * field)
        shrink = jnp.exp(-BETA * field)
        value = (
            panel(0) * field
            + near_value
            + panel(1) * (grow - shrink)
            + panel(2) * (field - panel(3))
            - source_term[...]
        )
        slope = panel(1) * (ALPHA * grow + BETA * shrink) + panel(2)
        return value, slope

    def apply_precond(value):
        high, low = halves(value)
        left = jnp.concatenate([high, low], axis=1)
        return jnp.stack([both_halves(left[b], precond_w[b]) for b in range(blocks)])

    field = potential0[...]
    near_now = near_field(0)
    for newton in range(NEWTON):
        turn = 1 + 2 * newton
        value, slope = mismatch(field, near_now)
        p0 = -value
        z0 = apply_precond(p0)
        start_exchange(turn, z0)
        diagonal = panel(0) + slope
        n0 = near_field(turn)
        p1 = diagonal * z0 + n0
        z1 = apply_precond(p1)
        start_exchange(turn + 1, z1)
        start_sums_a(2 * newton, [(p0, p0), (p0, p1)])
        start_sums_b(2 * newton)
        n1 = near_field(turn + 1)
        p2 = diagonal * z1 + n1
        g00, g01 = finish_sums(2 * newton, 2)
        beta2 = g00 + EPS
        h00 = g01 / beta2
        c = p1 - h00[None] * p0
        q = p2 - h00[None] * p1
        start_sums_a(2 * newton + 1, [(c, c), (p0, q), (c, q), (q, q)])
        start_sums_b(2 * newton + 1)
        cc, pq, cq, qq = finish_sums(2 * newton + 1, 4)
        beta = jnp.sqrt(beta2)
        pc = g01 - h00 * g00
        h10 = jnp.sqrt(cc / beta2 + EPS)
        scale = 1.0 / (beta * h10)
        scale2 = scale * scale
        v00 = g00 / beta2
        v01 = pc / beta * scale
        v11 = cc * scale2
        w0 = pq / beta * scale
        w1 = cq * scale2
        ww = qq * scale2
        h01 = w0
        h11 = w1 - h01 * v01
        square = (
            ww
            + h01 * h01 * v00
            + h11 * h11 * v11
            - 2.0 * h01 * w0
            - 2.0 * h11 * w1
            + 2.0 * h01 * h11 * v01
        )
        square = jnp.maximum(square, 0.0) + EPS
        gram0 = h00 * h00 + h10 * h10
        gram1 = h00 * h01 + h10 * h11
        gram2 = h01 * h01 + h11 * h11 + square
        lower0 = jnp.sqrt(gram0)
        lower1 = gram1 / lower0
        lower2 = jnp.sqrt(gram2 - lower1 * lower1)
        middle0 = beta * h00 / lower0
        middle1 = (beta * h01 - lower1 * middle0) / lower2
        y1 = middle1 / lower2
        y0 = (middle0 - lower1 * y1) / lower0
        a1 = y1 * scale
        a0 = y0 / beta - a1 * h00
        field = field + (a0[None] * z0 + a1[None] * z1)
        near_now = near_now + (a0[None] * n0 + a1[None] * n1)
    potential_o[...] = field
    residual_o[...] = mismatch(field, near_now)[0]

    for turn in range(2 * NEWTON + 1):
        exchange_copy(turn).wait_send()
    for turn in range(2 * NEWTON):
        sums_copy(0, turn).wait_send()
        sums_copy(1, turn).wait_send()


def body(patches, cols, potential0, source_term, self_coef, nearfield, precond, exch_current, conductance, member, anode_drive, pair_source, pair_count):
    blocks, columns, panels = potential0.shape
    pairs = nearfield.shape[1]
    turns = 2 * NEWTON + 1
    slots = (cols + 2) * blocks
    smem = pl.BlockSpec(memory_space=pltpu.SMEM)
    hbm = pl.BlockSpec(memory_space=pl.ANY)
    vmem = pl.BlockSpec(memory_space=pltpu.VMEM)
    out = jax.ShapeDtypeStruct((blocks, columns, panels), F32)
    return pl.pallas_call(
        functools.partial(kernel, patches, cols),
        out_shape=(out, out),
        in_specs=[smem] * 3 + [hbm] * 8,
        out_specs=(vmem, vmem),
        scratch_shapes=[
            pltpu.VMEM((blocks, columns, panels), F32),
            pltpu.VMEM((blocks, columns, panels), F32),
            pltpu.VMEM((4, blocks, panels), F32),
            pltpu.VMEM((blocks, panels), jnp.int32),
            pltpu.VMEM((blocks, pairs, panels, panels), F32),
            pltpu.VMEM((blocks, 2 * panels, pairs * panels), BF16),
            pltpu.VMEM((blocks, panels, panels), F32),
            pltpu.VMEM((blocks, 2 * panels, panels), BF16),
            pltpu.VMEM((turns, slots, columns, panels), F32),
            pltpu.VMEM((slots, 2 * columns, panels), BF16),
            pltpu.VMEM((blocks, columns, panels), F32),
            pltpu.VMEM((2 * NEWTON, patches, columns, 128), F32),
            pltpu.VMEM((2 * NEWTON, cols, columns, 128), F32),
            pltpu.SemaphoreType.DMA((7 + blocks,)),
            pltpu.SemaphoreType.DMA((turns,)),
            pltpu.SemaphoreType.DMA((turns,)),
            pltpu.SemaphoreType.DMA((2, 2 * NEWTON)),
            pltpu.SemaphoreType.DMA((2, 2 * NEWTON)),
        ],
        compiler_params=pltpu.CompilerParams(
            collective_id=0, has_side_effects=True, vmem_limit_bytes=40 * 1024 * 1024
        ),
        name="newton_gmres",
    )(
        anode_drive,
        pair_source,
        pair_count,
        potential0,
        source_term,
        self_coef,
        nearfield,
        precond,
        exch_current,
        conductance,
        member,
    )


def solution(mesh):
    both = ("patch", "col")
    return jax.shard_map(
        functools.partial(body, mesh.shape["patch"], mesh.shape["col"]),
        mesh=mesh,
        in_specs=(
            P(both, None, None),
            P(both, None, None),
            P(both, None),
            P(both, None, None, None),
            P(both, None, None),
            P(both, None),
            P(both, None),
            P(both, None),
            P(),
            P(both, None),
            P(both),
        ),
        out_specs=(P(both, None, None), P(both, None, None)),
        check_vma=False,
    )
```

```python
import functools

import jax
import jax.numpy as jnp
from jax import lax
from jax.experimental import pallas as pl
from jax.experimental.pallas import tpu as pltpu
from jax.sharding import PartitionSpec as P

NEWTON = 2

ALPHA = 0.6
BETA = 0.4
EPS = 1e-06

MESH = pl.DeviceIdType.MESH
F32 = jnp.float32
BF16 = jnp.bfloat16


def halves(array):
    high = array.astype(BF16)
    low = (array - high.astype(F32)).astype(BF16)
    return high, low


def both_halves(left, right):
    rows = left.shape[0] // 2
    wide = jnp.dot(left, right, preferred_element_type=F32)
    half = wide.shape[1] // 2
    return wide[:rows, :half] + (wide[rows:, :half] + wide[:rows, half:]) + wide[rows:, half:]


def kernel(
    patches,
    cols,
    drive_h,
    source_h,
    count_h,
    potential0_h,
    source_term_h,
    self_coef_h,
    nearfield_h,
    precond_h,
    current_h,
    conduct_h,
    member_h,
    potential_o,
    residual_o,
    drive_s,
    source_s,
    count_s,
    potential0,
    source_term,
    panels,
    member,
    staged,
    weights,
    precond_f,
    precond_w,
    exchange,
    split,
    sums,
    load_sem,
    send_sem,
    recv_sem,
    sum_send,
    sum_recv,
):
    patch = lax.axis_index("patch")
    col = lax.axis_index("col")
    blocks, pairs = source_s.shape
    columns = potential0.shape[1]
    slots = exchange.shape[1]

    loads = [
        pltpu.make_async_copy(potential0_h, potential0, load_sem.at[0]),
        pltpu.make_async_copy(source_term_h, source_term, load_sem.at[1]),
        pltpu.make_async_copy(self_coef_h, panels.at[0], load_sem.at[2]),
        pltpu.make_async_copy(current_h, panels.at[1], load_sem.at[3]),
        pltpu.make_async_copy(conduct_h, panels.at[2], load_sem.at[4]),
        pltpu.make_async_copy(member_h, member, load_sem.at[5]),
        pltpu.make_async_copy(precond_h, precond_f, load_sem.at[6]),
        pltpu.make_async_copy(drive_h, drive_s, load_sem.at[7]),
        pltpu.make_async_copy(source_h, source_s, load_sem.at[8]),
        pltpu.make_async_copy(count_h, count_s, load_sem.at[9]),
    ]
    matrix_loads = [
        pltpu.make_async_copy(nearfield_h.at[b], staged.at[b], load_sem.at[10 + b])
        for b in range(blocks)
    ]
    for load in loads + matrix_loads:
        load.start()

    me = patch * cols + col
    devices = patches * cols

    def peer_col(step):
        return lax.rem(col + step, cols)

    def peer_patch(step):
        return lax.rem(patch + step, patches)

    def everyone():
        def distance(step, size):
            return min(step, size - step)

        steps = [(p, c) for p in range(patches) for c in range(cols) if p or c]
        side = 4
        steps.sort(
            key=lambda s: (
                distance(s[0] // side, patches // side)
                + distance(s[0] % side, side)
                + distance(s[1] // 2, cols // 2)
            ),
            reverse=True,
        )
        near_patch = [peer_patch(p) for p in range(patches)]
        near_col = [peer_col(c) for c in range(cols)]
        return [(near_patch[p], near_col[c]) for p, c in steps]

    others = everyone()
    barrier = pltpu.get_barrier_semaphore()
    for target in others:
        pl.semaphore_signal(barrier, inc=1, device_id=target, device_id_type=MESH)
    pl.semaphore_wait(barrier, devices - 1)

    own = pl.ds(pl.multiple_of(col * blocks, blocks), blocks)
    before = pl.ds(cols * blocks, blocks)
    after = pl.ds((cols + 1) * blocks, blocks)
    incoming = pl.ds(0, slots - blocks)

    def start_exchange(turn, value):
        exchange[turn, own] = value
        mine = exchange.at[turn, own]

        def send(place, target):
            pltpu.make_async_remote_copy(
                src_ref=mine,
                dst_ref=exchange.at[turn, place],
                send_sem=send_sem.at[turn],
                recv_sem=recv_sem.at[turn],
                device_id=target,
                device_id_type=MESH,
            ).start()

        steps = sorted(range(1, cols), key=lambda s: -min(s // 2, cols // 2 - s // 2))
        for step in steps:
            send(own, {"col": peer_col(step)})
        send(before, {"patch": peer_patch(1)})
        send(after, {"patch": peer_patch(patches - 1)})

    def exchange_copy(turn):
        return pltpu.make_async_remote_copy(
            src_ref=exchange.at[turn, incoming],
            dst_ref=exchange.at[turn, incoming],
            send_sem=send_sem.at[turn],
            recv_sem=recv_sem.at[turn],
            device_id={"col": peer_col(1)},
            device_id_type=MESH,
        )

    def near_field(turn):
        exchange_copy(turn).wait_recv()
        high, low = halves(exchange[turn])
        split[:, :columns] = high
        split[:, columns:] = low

        results = []
        for b in range(blocks):
            left = jnp.concatenate([split[source_s[b, k]] for k in range(pairs)], axis=1)
            results.append(both_halves(left, weights[b]))
        return jnp.stack(results)

    def start_sums(turn, parts):
        rows = [jnp.sum(left * right, axis=0) for left, right in parts]
        rows.append(jnp.zeros((128 - len(parts) * columns, 128), F32))
        table = jnp.concatenate(rows, axis=0)
        sums[turn, me] = jnp.sum(table.T, axis=0, keepdims=True)
        for target in others:
            pltpu.make_async_remote_copy(
                src_ref=sums.at[turn, me],
                dst_ref=sums.at[turn, me],
                send_sem=sum_send.at[turn],
                recv_sem=sum_recv.at[turn],
                device_id=target,
                device_id_type=MESH,
            ).start()

    def sums_copy(turn):
        rest = sums.at[turn, pl.ds(0, devices - 1)]
        return pltpu.make_async_remote_copy(
            src_ref=rest,
            dst_ref=rest,
            send_sem=sum_send.at[turn],
            recv_sem=sum_recv.at[turn],
            device_id={"col": peer_col(1)},
            device_id_type=MESH,
        )

    def finish_sums(turn, count):
        sums_copy(turn).wait_recv()
        total = jnp.broadcast_to(jnp.sum(sums[turn], axis=0), (8, 128))
        return [
            total if place == 0 else pltpu.roll(total, 128 - place * columns, 1)
            for place in range(count)
        ]

    lane = lax.broadcasted_iota(jnp.int32, (columns, 128), 1)
    row = lax.broadcasted_iota(jnp.int32, (columns, 128), 0)

    def by_column(lanes):
        wide = jnp.broadcast_to(lanes[:1], (columns, 128))
        picked = jnp.sum(jnp.where(lane == row, wide, 0.0), axis=1, keepdims=True)
        return jnp.broadcast_to(picked, (columns, 128))[None]

    loads[0].wait()
    start_exchange(0, potential0[...])
    for load in loads[1:]:
        load.wait()

    owner = member[...]
    drive = jnp.zeros(owner.shape, F32)
    for place in range(drive_s.shape[0]):
        drive = jnp.where(owner == place, drive_s[place], drive)
    panels[3] = drive
    for b in range(blocks):
        high, low = halves(precond_f[b].T)
        precond_w[b, :, :128] = high
        precond_w[b, :, 128:] = low

    for b in range(blocks):
        matrix_loads[b].wait()

        def prepare(k, carry, b=b):
            live = jnp.where(k < count_s[b], 1.0, 0.0).astype(F32)
            high, low = halves((staged[b, k] * live).T)
            place = pl.ds(pl.multiple_of(k * 128, 128), 128)
            weights[b, place, :128] = high
            weights[b, place, 128:] = low
            return carry

        lax.fori_loop(0, pairs, prepare, 0, unroll=4)

    def panel(place):
        return panels[place][:, None, :]

    def mismatch(field, near_value):
        grow = jnp.exp(ALPHA * field)
        shrink = jnp.exp(-BETA * field)
        value = (
            panel(0) * field
            + near_value
            + panel(1) * (grow - shrink)
            + panel(2) * (field - panel(3))
            - source_term[...]
        )
        slope = panel(1) * (ALPHA * grow + BETA * shrink) + panel(2)
        return value, slope

    def apply_precond(value):
        high, low = halves(value)
        left = jnp.concatenate([high, low], axis=1)
        return jnp.stack([both_halves(left[b], precond_w[b]) for b in range(blocks)])

    field = potential0[...]
    near_now = near_field(0)
    for newton in range(NEWTON):
        turn = 1 + 2 * newton
        value, slope = mismatch(field, near_now)
        p0 = -value
        z0 = apply_precond(p0)
        start_exchange(turn, z0)
        start_sums(2 * newton, [(p0, p0)])
        diagonal = panel(0) + slope
        n0 = near_field(turn)
        (g00,) = finish_sums(2 * newton, 1)
        beta2 = g00 + EPS
        beta = jnp.sqrt(beta2)
        unit = by_column(1.0 / beta)
        v0 = p0 * unit
        z0 = z0 * unit
        n0 = n0 * unit
        p1 = diagonal * z0 + n0
        z1 = apply_precond(p1)
        start_exchange(turn + 1, z1)
        n1 = near_field(turn + 1)
        p2 = diagonal * z1 + n1
        start_sums(
            2 * newton + 1, [(v0, p1), (p1, p1), (v0, p2), (p1, p2), (p2, p2)]
        )
        h00, g11, g02, g12, g22 = finish_sums(2 * newton + 1, 5)
        v00 = g00 / beta2
        pc = h00 - h00 * v00
        cc = jnp.maximum(g11 - h00 * h00 - h00 * pc, 0.0)
        pq = g02 - h00 * h00
        cq = g12 - h00 * g02 - h00 * (g11 - h00 * h00)
        qq = jnp.maximum(g22 - h00 * (2.0 * g12 - h00 * g11), 0.0)
        h10 = jnp.sqrt(cc + EPS)
        scale = 1.0 / h10
        scale2 = scale * scale
        v01 = pc * scale
        v11 = cc * scale2
        h01 = pq * scale
        w1 = cq * scale2
        h11 = w1 - h01 * v01
        square = (
            qq * scale2
            + h01 * h01 * v00
            + h11 * h11 * v11
            - 2.0 * h01 * h01
            - 2.0 * h11 * w1
            + 2.0 * h01 * h11 * v01
        )
        square = jnp.maximum(square, 0.0) + EPS
        gram0 = h00 * h00 + h10 * h10
        gram1 = h00 * h01 + h10 * h11
        gram2 = h01 * h01 + h11 * h11 + square
        lower0 = jnp.sqrt(gram0)
        lower1 = gram1 / lower0
        lower2 = jnp.sqrt(gram2 - lower1 * lower1)
        middle0 = beta * h00 / lower0
        middle1 = (beta * h01 - lower1 * middle0) / lower2
        y1 = middle1 / lower2
        y0 = (middle0 - lower1 * y1) / lower0
        a1 = y1 * scale
        a0 = by_column(y0 - a1 * h00)
        a1 = by_column(a1)
        field = field + (a0 * z0 + a1 * z1)
        near_now = near_now + (a0 * n0 + a1 * n1)
    potential_o[...] = field
    residual_o[...] = mismatch(field, near_now)[0]

    for turn in range(2 * NEWTON + 1):
        exchange_copy(turn).wait_send()
    for turn in range(2 * NEWTON):
        sums_copy(turn).wait_send()


def body(patches, cols, potential0, source_term, self_coef, nearfield, precond, exch_current, conductance, member, anode_drive, pair_source, pair_count):
    blocks, columns, panels = potential0.shape
    pairs = nearfield.shape[1]
    turns = 2 * NEWTON + 1
    slots = (cols + 2) * blocks
    hbm = pl.BlockSpec(memory_space=pltpu.HBM)
    vmem = pl.BlockSpec(memory_space=pltpu.VMEM)
    out = jax.ShapeDtypeStruct((blocks, columns, panels), F32)
    return pl.pallas_call(
        functools.partial(kernel, patches, cols),
        out_shape=(out, out),
        in_specs=[hbm] * 11,
        out_specs=(vmem, vmem),
        scratch_shapes=[
            pltpu.SMEM(anode_drive.shape, F32),
            pltpu.SMEM(pair_source.shape, jnp.int32),
            pltpu.SMEM(pair_count.shape, jnp.int32),
            pltpu.VMEM((blocks, columns, panels), F32),
            pltpu.VMEM((blocks, columns, panels), F32),
            pltpu.VMEM((4, blocks, panels), F32),
            pltpu.VMEM((blocks, panels), jnp.int32),
            pltpu.VMEM((blocks, pairs, panels, panels), F32),
            pltpu.VMEM((blocks, pairs * panels, 2 * panels), BF16),
            pltpu.VMEM((blocks, panels, panels), F32),
            pltpu.VMEM((blocks, panels, 2 * panels), BF16),
            pltpu.VMEM((turns, slots, columns, panels), F32),
            pltpu.VMEM((slots, 2 * columns, panels), BF16),
            pltpu.VMEM((2 * NEWTON, patches * cols, 1, 128), F32),
            pltpu.SemaphoreType.DMA((10 + blocks,)),
            pltpu.SemaphoreType.DMA((turns,)),
            pltpu.SemaphoreType.DMA((turns,)),
            pltpu.SemaphoreType.DMA((2 * NEWTON,)),
            pltpu.SemaphoreType.DMA((2 * NEWTON,)),
        ],
        compiler_params=pltpu.CompilerParams(
            collective_id=0, has_side_effects=True, vmem_limit_bytes=40 * 1024 * 1024
        ),
        name="newton_gmres",
    )(
        *(
            pltpu.with_memory_space_constraint(array, pltpu.HBM)
            for array in (
                anode_drive,
                pair_source,
                pair_count,
                potential0,
                source_term,
                self_coef,
                nearfield,
                precond,
                exch_current,
                conductance,
                member,
            )
        )
    )


def solution(mesh):
    both = ("patch", "col")
    return jax.shard_map(
        functools.partial(body, mesh.shape["patch"], mesh.shape["col"]),
        mesh=mesh,
        in_specs=(
            P(both, None, None),
            P(both, None, None),
            P(both, None),
            P(both, None, None, None),
            P(both, None, None),
            P(both, None),
            P(both, None),
            P(both, None),
            P(),
            P(both, None),
            P(both),
        ),
        out_specs=(P(both, None, None), P(both, None, None)),
        check_vma=False,
    )
```

```python
import functools

import jax
import jax.numpy as jnp
from jax import lax
from jax.experimental import pallas as pl
from jax.experimental.pallas import tpu as pltpu
from jax.sharding import PartitionSpec as P

NEWTON = 2

ALPHA = 0.6
BETA = 0.4
EPS = 1e-06

MESH = pl.DeviceIdType.MESH
F32 = jnp.float32
BF16 = jnp.bfloat16


def halves(array):
    high = array.astype(BF16)
    low = (array - high.astype(F32)).astype(BF16)
    return high, low


def both_halves(left, right):
    rows = left.shape[0] // 2
    wide = jnp.dot(left, right, preferred_element_type=F32)
    half = wide.shape[1] // 2
    return wide[:rows, :half] + (wide[rows:, :half] + wide[:rows, half:]) + wide[rows:, half:]


def kernel(
    patches,
    cols,
    drive_h,
    source_h,
    count_h,
    potential0_h,
    source_term_h,
    self_coef_h,
    nearfield_h,
    precond_h,
    current_h,
    conduct_h,
    member_h,
    both_o,
    drive_s,
    source_s,
    count_s,
    potential0,
    source_term,
    panels,
    member,
    staged,
    weights,
    precond_f,
    precond_w,
    exchange,
    split,
    sums,
    load_sem,
    send_sem,
    recv_sem,
    sum_sem,
    beta_a,
    beta_b,
    beta_sem,
    entered_sem,
):
    patch = lax.axis_index("patch")
    col = lax.axis_index("col")
    blocks, pairs = source_s.shape
    columns = potential0.shape[1]
    slots = exchange.shape[1]

    loads = [
        pltpu.make_async_copy(potential0_h, potential0, load_sem.at[0]),
        pltpu.make_async_copy(source_term_h, source_term, load_sem.at[1]),
        pltpu.make_async_copy(self_coef_h, panels.at[0], load_sem.at[2]),
        pltpu.make_async_copy(current_h, panels.at[1], load_sem.at[3]),
        pltpu.make_async_copy(conduct_h, panels.at[2], load_sem.at[4]),
        pltpu.make_async_copy(member_h, member, load_sem.at[5]),
        pltpu.make_async_copy(precond_h, precond_f, load_sem.at[6]),
        pltpu.make_async_copy(drive_h, drive_s, load_sem.at[7]),
        pltpu.make_async_copy(source_h, source_s, load_sem.at[8]),
        pltpu.make_async_copy(count_h, count_s, load_sem.at[9]),
    ]
    matrix_loads = [
        pltpu.make_async_copy(nearfield_h.at[b], staged.at[b], load_sem.at[10 + b])
        for b in range(blocks)
    ]
    for load in loads + matrix_loads:
        load.start()

    me = patch * cols + col
    devices = patches * cols

    def peer_col(step):
        return lax.rem(col + step, cols)

    def peer_patch(step):
        return lax.rem(patch + step, patches)

    def everyone():
        def distance(step, size):
            return min(step, size - step)

        steps = [(p, c) for p in range(patches) for c in range(cols) if p or c]
        side = 4
        steps.sort(
            key=lambda s: (
                distance(s[0] // side, patches // side)
                + distance(s[0] % side, side)
                + distance(s[1] // 2, cols // 2)
            ),
            reverse=True,
        )
        near_patch = [peer_patch(p) for p in range(patches)]
        near_col = [peer_col(c) for c in range(cols)]
        return [(near_patch[p], near_col[c]) for p, c in steps]

    others = everyone()
    side = 4
    line, place = patch // side, lax.rem(patch, side)
    col_peers = [{"col": peer_col(step)} for step in range(1, cols)]
    y_peers = [
        {"patch": lax.rem(line + step, patches // side) * side + place}
        for step in range(1, patches // side)
    ]
    x_peers = [{"patch": line * side + lax.rem(place + step, side)} for step in range(1, side)]
    next_peers = [{"patch": peer_patch(1)}, {"patch": peer_patch(patches - 1)}]

    def signal_all(semaphore, targets):
        for target in targets:
            pl.semaphore_signal(semaphore, inc=1, device_id=target, device_id_type=MESH)

    barrier = pltpu.get_barrier_semaphore()
    greeted = x_peers + y_peers + next_peers + col_peers
    signal_all(barrier, greeted)
    pl.semaphore_wait(barrier, len(greeted))

    own = pl.ds(pl.multiple_of(col * blocks, blocks), blocks)
    before = pl.ds(cols * blocks, blocks)
    after = pl.ds((cols + 1) * blocks, blocks)
    incoming = pl.ds(0, slots - blocks)

    def start_exchange(turn, value):
        exchange[turn, own] = value
        mine = exchange.at[turn, own]

        def send(place, target):
            pltpu.make_async_remote_copy(
                src_ref=mine,
                dst_ref=exchange.at[turn, place],
                send_sem=send_sem.at[turn],
                recv_sem=recv_sem.at[turn],
                device_id=target,
                device_id_type=MESH,
            ).start()

        steps = sorted(range(1, cols), key=lambda s: -min(s // 2, cols // 2 - s // 2))
        for step in steps:
            send(own, {"col": peer_col(step)})
        send(before, {"patch": peer_patch(1)})
        send(after, {"patch": peer_patch(patches - 1)})

    def exchange_copy(turn):
        return pltpu.make_async_remote_copy(
            src_ref=exchange.at[turn, incoming],
            dst_ref=exchange.at[turn, incoming],
            send_sem=send_sem.at[turn],
            recv_sem=recv_sem.at[turn],
            device_id={"col": peer_col(1)},
            device_id_type=MESH,
        )

    def near_field(turn):
        exchange_copy(turn).wait_recv()
        high, low = halves(exchange[turn])
        split[:, :columns] = high
        split[:, columns:] = low

        results = []
        for b in range(blocks):
            left = jnp.concatenate([split[source_s[b, k]] for k in range(pairs)], axis=1)
            results.append(both_halves(left, weights[b]))
        return jnp.stack(results)

    def spread(buffer, mine, semaphores, targets):
        for target in targets:
            pltpu.make_async_remote_copy(
                src_ref=buffer.at[mine],
                dst_ref=buffer.at[mine],
                send_sem=semaphores.at[0],
                recv_sem=semaphores.at[1],
                device_id=target,
                device_id_type=MESH,
            ).start()

    def spread_copy(buffer, semaphores):
        rest = buffer.at[pl.ds(0, buffer.shape[0] - 1)]
        return pltpu.make_async_remote_copy(
            src_ref=rest,
            dst_ref=rest,
            send_sem=semaphores.at[0],
            recv_sem=semaphores.at[1],
            device_id={"col": peer_col(1)},
            device_id_type=MESH,
        )

    patch_peers = [{"patch": peer_patch(step)} for step in range(1, patches)]

    def start_beta(newton, value):
        table = jnp.concatenate(
            [jnp.sum(value * value, axis=0), jnp.zeros((128 - columns, 128), F32)], axis=0
        )
        beta_a[newton, patch] = jnp.sum(table.T, axis=0, keepdims=True)
        spread(beta_a.at[newton], patch, beta_sem.at[newton, 0], patch_peers)

    def pass_beta(newton):
        spread_copy(beta_a.at[newton], beta_sem.at[newton, 0]).wait_recv()
        beta_b[newton, col] = jnp.sum(beta_a[newton], axis=0)
        spread(beta_b.at[newton], col, beta_sem.at[newton, 1], col_peers)

    def finish_beta(newton):
        spread_copy(beta_b.at[newton], beta_sem.at[newton, 1]).wait_recv()
        return jnp.broadcast_to(jnp.sum(beta_b[newton], axis=0), (8, 128))

    def start_sums(turn, parts):
        rows = [jnp.sum(left * right, axis=0) for left, right in parts]
        rows.append(jnp.zeros((128 - len(parts) * columns, 128), F32))
        table = jnp.concatenate(rows, axis=0)
        sums[turn, me] = jnp.sum(table.T, axis=0, keepdims=True)
        spread(sums.at[turn], me, sum_sem.at[turn], others)

    def finish_sums(turn, count):
        spread_copy(sums.at[turn], sum_sem.at[turn]).wait_recv()
        total = jnp.broadcast_to(jnp.sum(sums[turn], axis=0), (8, 128))
        return [
            total if place == 0 else pltpu.roll(total, 128 - place * columns, 1)
            for place in range(count)
        ]

    lane = lax.broadcasted_iota(jnp.int32, (columns, 128), 1)
    row = lax.broadcasted_iota(jnp.int32, (columns, 128), 0)

    def by_column(lanes):
        wide = jnp.broadcast_to(lanes[:1], (columns, 128))
        picked = jnp.sum(jnp.where(lane == row, wide, 0.0), axis=1, keepdims=True)
        return jnp.broadcast_to(picked, (columns, 128))[None]

    loads[0].wait()
    start_exchange(0, potential0[...])
    signal_all(entered_sem.at[0], x_peers)
    for load in loads[1:]:
        load.wait()

    owner = member[...]
    drive = jnp.zeros(owner.shape, F32)
    for place in range(drive_s.shape[0]):
        drive = jnp.where(owner == place, drive_s[place], drive)
    panels[3] = drive
    for b in range(blocks):
        high, low = halves(precond_f[b].T)
        precond_w[b, :, :128] = high
        precond_w[b, :, 128:] = low

    for b in range(blocks):
        matrix_loads[b].wait()

        def prepare(k, carry, b=b):
            live = jnp.where(k < count_s[b], 1.0, 0.0).astype(F32)
            high, low = halves((staged[b, k] * live).T)
            place = pl.ds(pl.multiple_of(k * 128, 128), 128)
            weights[b, place, :128] = high
            weights[b, place, 128:] = low
            return carry

        lax.fori_loop(0, pairs, prepare, 0, unroll=4)

    def panel(place):
        return panels[place][:, None, :]

    def mismatch(field, near_value):
        grow = jnp.exp(ALPHA * field)
        shrink = jnp.exp(-BETA * field)
        value = (
            panel(0) * field
            + near_value
            + panel(1) * (grow - shrink)
            + panel(2) * (field - panel(3))
            - source_term[...]
        )
        slope = panel(1) * (ALPHA * grow + BETA * shrink) + panel(2)
        return value, slope

    def apply_precond(value):
        high, low = halves(value)
        left = jnp.concatenate([high, low], axis=1)
        return jnp.stack([both_halves(left[b], precond_w[b]) for b in range(blocks)])

    pl.semaphore_wait(entered_sem.at[0], len(x_peers))
    signal_all(entered_sem.at[1], col_peers)
    field = potential0[...]
    near_now = near_field(0)
    pl.semaphore_wait(entered_sem.at[1], len(col_peers))
    for newton in range(NEWTON):
        turn = 1 + 2 * newton
        value, slope = mismatch(field, near_now)
        p0 = -value
        z0 = apply_precond(p0)
        start_exchange(turn, z0)
        start_beta(newton, p0)
        diagonal = panel(0) + slope
        n0 = near_field(turn)
        p1 = diagonal * z0 + n0
        z1 = apply_precond(p1)
        start_exchange(turn + 1, z1)
        pass_beta(newton)
        n1 = near_field(turn + 1)
        p2 = diagonal * z1 + n1
        g00 = finish_beta(newton)
        beta2 = g00 + EPS
        beta = jnp.sqrt(beta2)
        unit = by_column(1.0 / beta)
        v0, p1, p2 = p0 * unit, p1 * unit, p2 * unit
        start_sums(
            newton, [(v0, p1), (p1, p1), (v0, p2), (p1, p2), (p2, p2)]
        )
        h00, g11, g02, g12, g22 = finish_sums(newton, 5)
        v00 = g00 / beta2
        pc = h00 - h00 * v00
        cc = jnp.maximum(g11 - h00 * h00 - h00 * pc, 0.0)
        pq = g02 - h00 * h00
        cq = g12 - h00 * g02 - h00 * (g11 - h00 * h00)
        qq = jnp.maximum(g22 - h00 * (2.0 * g12 - h00 * g11), 0.0)
        h10 = jnp.sqrt(cc + EPS)
        scale = 1.0 / h10
        scale2 = scale * scale
        v01 = pc * scale
        v11 = cc * scale2
        h01 = pq * scale
        w1 = cq * scale2
        h11 = w1 - h01 * v01
        square = (
            qq * scale2
            + h01 * h01 * v00
            + h11 * h11 * v11
            - 2.0 * h01 * h01
            - 2.0 * h11 * w1
            + 2.0 * h01 * h11 * v01
        )
        square = jnp.maximum(square, 0.0) + EPS
        gram0 = h00 * h00 + h10 * h10
        gram1 = h00 * h01 + h10 * h11
        gram2 = h01 * h01 + h11 * h11 + square
        lower0 = jnp.sqrt(gram0)
        lower1 = gram1 / lower0
        lower2 = jnp.sqrt(gram2 - lower1 * lower1)
        middle0 = beta * h00 / lower0
        middle1 = (beta * h01 - lower1 * middle0) / lower2
        y1 = middle1 / lower2
        y0 = (middle0 - lower1 * y1) / lower0
        a1 = y1 * scale
        a0 = by_column((y0 - a1 * h00) / beta)
        a1 = by_column(a1 / beta)
        field = field + (a0 * z0 + a1 * z1)
        near_now = near_now + (a0 * n0 + a1 * n1)
    both_o[0] = field
    both_o[1] = mismatch(field, near_now)[0]

    for turn in range(2 * NEWTON + 1):
        exchange_copy(turn).wait_send()
    for newton in range(NEWTON):
        spread_copy(sums.at[newton], sum_sem.at[newton]).wait_send()
        spread_copy(beta_a.at[newton], beta_sem.at[newton, 0]).wait_send()
        spread_copy(beta_b.at[newton], beta_sem.at[newton, 1]).wait_send()


def body(patches, cols, potential0, source_term, self_coef, nearfield, precond, exch_current, conductance, member, anode_drive, pair_source, pair_count):
    blocks, columns, panels = potential0.shape
    pairs = nearfield.shape[1]
    turns = 2 * NEWTON + 1
    slots = (cols + 2) * blocks
    hbm = pl.BlockSpec(memory_space=pltpu.HBM)
    vmem = pl.BlockSpec(memory_space=pltpu.VMEM)
    out = jax.ShapeDtypeStruct((2, blocks, columns, panels), F32)
    both = pl.pallas_call(
        functools.partial(kernel, patches, cols),
        out_shape=out,
        in_specs=[hbm] * 11,
        out_specs=vmem,
        scratch_shapes=[
            pltpu.SMEM(anode_drive.shape, F32),
            pltpu.SMEM(pair_source.shape, jnp.int32),
            pltpu.SMEM(pair_count.shape, jnp.int32),
            pltpu.VMEM((blocks, columns, panels), F32),
            pltpu.VMEM((blocks, columns, panels), F32),
            pltpu.VMEM((4, blocks, panels), F32),
            pltpu.VMEM((blocks, panels), jnp.int32),
            pltpu.VMEM((blocks, pairs, panels, panels), F32),
            pltpu.VMEM((blocks, pairs * panels, 2 * panels), BF16),
            pltpu.VMEM((blocks, panels, panels), F32),
            pltpu.VMEM((blocks, panels, 2 * panels), BF16),
            pltpu.VMEM((turns, slots, columns, panels), F32),
            pltpu.VMEM((slots, 2 * columns, panels), BF16),
            pltpu.VMEM((NEWTON, patches * cols, 1, 128), F32),
            pltpu.SemaphoreType.DMA((10 + blocks,)),
            pltpu.SemaphoreType.DMA((turns,)),
            pltpu.SemaphoreType.DMA((turns,)),
            pltpu.SemaphoreType.DMA((NEWTON, 2)),
            pltpu.VMEM((NEWTON, patches, 1, 128), F32),
            pltpu.VMEM((NEWTON, cols, 1, 128), F32),
            pltpu.SemaphoreType.DMA((NEWTON, 2, 2)),
            pltpu.SemaphoreType.REGULAR((2,)),
        ],
        compiler_params=pltpu.CompilerParams(
            collective_id=0, has_side_effects=True, vmem_limit_bytes=40 * 1024 * 1024
        ),
        name="newton_gmres",
    )(
        *(
            pltpu.with_memory_space_constraint(array, pltpu.HBM)
            for array in (
                anode_drive,
                pair_source,
                pair_count,
                potential0,
                source_term,
                self_coef,
                nearfield,
                precond,
                exch_current,
                conductance,
                member,
            )
        )
    )
    return both[0], both[1]


def solution(mesh):
    both = ("patch", "col")
    return jax.shard_map(
        functools.partial(body, mesh.shape["patch"], mesh.shape["col"]),
        mesh=mesh,
        in_specs=(
            P(both, None, None),
            P(both, None, None),
            P(both, None),
            P(both, None, None, None),
            P(both, None, None),
            P(both, None),
            P(both, None),
            P(both, None),
            P(),
            P(both, None),
            P(both),
        ),
        out_specs=(P(both, None, None), P(both, None, None)),
        check_vma=False,
    )
```

```python
import functools

import jax
import jax.numpy as jnp
from jax import lax
from jax.experimental import pallas as pl
from jax.experimental.pallas import tpu as pltpu
from jax.sharding import PartitionSpec as P

NEWTON = 2

ALPHA = 0.6
BETA = 0.4
EPS = 1e-06

MESH = pl.DeviceIdType.MESH
F32 = jnp.float32
BF16 = jnp.bfloat16


def halves(array):
    high = array.astype(BF16)
    low = (array - high.astype(F32)).astype(BF16)
    return high, low


def both_halves(left, right):
    rows = left.shape[0] // 2
    wide = jnp.dot(left, right, preferred_element_type=F32)
    half = wide.shape[1] // 2
    return wide[:rows, :half] + (wide[rows:, :half] + wide[:rows, half:]) + wide[rows:, half:]


def kernel(
    patches,
    cols,
    drive_h,
    source_h,
    count_h,
    potential0_h,
    source_term_h,
    self_coef_h,
    nearfield_h,
    precond_h,
    current_h,
    conduct_h,
    member_h,
    both_o,
    drive_s,
    source_s,
    count_s,
    potential0,
    source_term,
    panels,
    member,
    staged,
    weights,
    precond_f,
    precond_w,
    exchange,
    split,
    sums,
    load_sem,
    send_sem,
    recv_sem,
    sum_sem,
    beta_a,
    beta_b,
    beta_sem,
    entered_sem,
):
    patch = lax.axis_index("patch")
    col = lax.axis_index("col")
    blocks, pairs = source_s.shape
    columns = potential0.shape[1]
    slots = exchange.shape[1]

    me = patch * cols + col
    devices = patches * cols

    def peer_col(step):
        return lax.rem(col + step, cols)

    def peer_patch(step):
        return lax.rem(patch + step, patches)

    def everyone():
        def distance(step, size):
            return min(step, size - step)

        steps = [(p, c) for p in range(patches) for c in range(cols) if p or c]
        side = 4
        steps.sort(
            key=lambda s: (
                distance(s[0] // side, patches // side)
                + distance(s[0] % side, side)
                + distance(s[1] // 2, cols // 2)
            ),
            reverse=True,
        )
        near_patch = [peer_patch(p) for p in range(patches)]
        near_col = [peer_col(c) for c in range(cols)]
        return [(near_patch[p], near_col[c]) for p, c in steps]

    others = everyone()
    side = 4
    line, place = patch // side, lax.rem(patch, side)
    col_peers = [{"col": peer_col(step)} for step in range(1, cols)]
    y_peers = [
        {"patch": lax.rem(line + step, patches // side) * side + place}
        for step in range(1, patches // side)
    ]
    x_peers = [{"patch": line * side + lax.rem(place + step, side)} for step in range(1, side)]
    next_peers = [{"patch": peer_patch(1)}, {"patch": peer_patch(patches - 1)}]

    def signal_all(semaphore, targets):
        for target in targets:
            pl.semaphore_signal(semaphore, inc=1, device_id=target, device_id_type=MESH)

    barrier = pltpu.get_barrier_semaphore()
    greeted = x_peers + y_peers + next_peers + col_peers
    signal_all(barrier, greeted)

    loads = [
        pltpu.make_async_copy(potential0_h, potential0, load_sem.at[0]),
        pltpu.make_async_copy(source_term_h, source_term, load_sem.at[1]),
        pltpu.make_async_copy(self_coef_h, panels.at[0], load_sem.at[2]),
        pltpu.make_async_copy(current_h, panels.at[1], load_sem.at[3]),
        pltpu.make_async_copy(conduct_h, panels.at[2], load_sem.at[4]),
        pltpu.make_async_copy(member_h, member, load_sem.at[5]),
        pltpu.make_async_copy(precond_h, precond_f, load_sem.at[6]),
        pltpu.make_async_copy(drive_h, drive_s, load_sem.at[7]),
        pltpu.make_async_copy(source_h, source_s, load_sem.at[8]),
        pltpu.make_async_copy(count_h, count_s, load_sem.at[9]),
    ]
    matrix_loads = [
        pltpu.make_async_copy(nearfield_h.at[b], staged.at[b], load_sem.at[10 + b])
        for b in range(blocks)
    ]
    for load in loads + matrix_loads:
        load.start()

    pl.semaphore_wait(barrier, len(greeted))

    own = pl.ds(pl.multiple_of(col * blocks, blocks), blocks)
    before = pl.ds(cols * blocks, blocks)
    after = pl.ds((cols + 1) * blocks, blocks)
    incoming = pl.ds(0, slots - blocks)

    def start_exchange(turn, value):
        exchange[turn, own] = value
        mine = exchange.at[turn, own]

        def send(place, target):
            pltpu.make_async_remote_copy(
                src_ref=mine,
                dst_ref=exchange.at[turn, place],
                send_sem=send_sem.at[turn],
                recv_sem=recv_sem.at[turn],
                device_id=target,
                device_id_type=MESH,
            ).start()

        steps = sorted(range(1, cols), key=lambda s: -min(s // 2, cols // 2 - s // 2))
        for step in steps:
            send(own, {"col": peer_col(step)})
        send(before, {"patch": peer_patch(1)})
        send(after, {"patch": peer_patch(patches - 1)})

    def exchange_copy(turn):
        return pltpu.make_async_remote_copy(
            src_ref=exchange.at[turn, incoming],
            dst_ref=exchange.at[turn, incoming],
            send_sem=send_sem.at[turn],
            recv_sem=recv_sem.at[turn],
            device_id={"col": peer_col(1)},
            device_id_type=MESH,
        )

    def near_field(turn, then=lambda: None):
        exchange_copy(turn).wait_recv()
        then()
        high, low = halves(exchange[turn])
        split[:, :columns] = high
        split[:, columns:] = low

        results = []
        for b in range(blocks):
            left = jnp.concatenate([split[source_s[b, k]] for k in range(pairs)], axis=1)
            results.append(both_halves(left, weights[b]))
        return jnp.stack(results)

    def spread(buffer, mine, semaphores, targets):
        for target in targets:
            pltpu.make_async_remote_copy(
                src_ref=buffer.at[mine],
                dst_ref=buffer.at[mine],
                send_sem=semaphores.at[0],
                recv_sem=semaphores.at[1],
                device_id=target,
                device_id_type=MESH,
            ).start()

    def spread_copy(buffer, semaphores):
        rest = buffer.at[pl.ds(0, buffer.shape[0] - 1)]
        return pltpu.make_async_remote_copy(
            src_ref=rest,
            dst_ref=rest,
            send_sem=semaphores.at[0],
            recv_sem=semaphores.at[1],
            device_id={"col": peer_col(1)},
            device_id_type=MESH,
        )

    patch_peers = [{"patch": peer_patch(step)} for step in range(1, patches)]

    def start_beta(newton, value):
        table = jnp.concatenate(
            [jnp.sum(value * value, axis=0), jnp.zeros((128 - columns, 128), F32)], axis=0
        )
        beta_a[newton, patch] = jnp.sum(table.T, axis=0, keepdims=True)
        spread(beta_a.at[newton], patch, beta_sem.at[newton, 0], patch_peers)

    def pass_beta(newton):
        spread_copy(beta_a.at[newton], beta_sem.at[newton, 0]).wait_recv()
        beta_b[newton, col] = jnp.sum(beta_a[newton], axis=0)
        spread(beta_b.at[newton], col, beta_sem.at[newton, 1], col_peers)

    def finish_beta(newton):
        spread_copy(beta_b.at[newton], beta_sem.at[newton, 1]).wait_recv()
        return jnp.broadcast_to(jnp.sum(beta_b[newton], axis=0), (8, 128))

    def products(left, right):
        return jnp.sum(left * right, axis=0)

    def start_sums(turn, parts):
        rest = jnp.zeros((128 - len(parts) * columns, 128), F32)
        table = jnp.concatenate(parts + [rest], axis=0)
        sums[turn, me] = jnp.sum(table.T, axis=0, keepdims=True)
        spread(sums.at[turn], me, sum_sem.at[turn], others)

    def finish_sums(turn, count):
        spread_copy(sums.at[turn], sum_sem.at[turn]).wait_recv()
        total = jnp.broadcast_to(jnp.sum(sums[turn], axis=0), (8, 128))
        return [
            total if place == 0 else pltpu.roll(total, 128 - place * columns, 1)
            for place in range(count)
        ]

    lane = lax.broadcasted_iota(jnp.int32, (columns, 128), 1)
    row = lax.broadcasted_iota(jnp.int32, (columns, 128), 0)

    def by_column(lanes):
        wide = jnp.broadcast_to(lanes[:1], (columns, 128))
        picked = jnp.sum(jnp.where(lane == row, wide, 0.0), axis=1, keepdims=True)
        return jnp.broadcast_to(picked, (columns, 128))[None]

    loads[0].wait()
    start_exchange(0, potential0[...])
    signal_all(entered_sem.at[0], x_peers)
    for load in loads[1:]:
        load.wait()

    owner = member[...]
    drive = jnp.zeros(owner.shape, F32)
    for place in range(drive_s.shape[0]):
        drive = jnp.where(owner == place, drive_s[place], drive)
    panels[3] = drive
    for b in range(blocks):
        high, low = halves(precond_f[b].T)
        precond_w[b, :, :128] = high
        precond_w[b, :, 128:] = low

    for b in range(blocks):
        matrix_loads[b].wait()

        def prepare(k, carry, b=b):
            live = jnp.where(k < count_s[b], 1.0, 0.0).astype(F32)
            high, low = halves((staged[b, k] * live).T)
            place = pl.ds(pl.multiple_of(k * 128, 128), 128)
            weights[b, place, :128] = high
            weights[b, place, 128:] = low
            return carry

        lax.fori_loop(0, pairs, prepare, 0, unroll=4)

    def panel(place):
        return panels[place][:, None, :]

    def mismatch(field, near_value):
        grow = jnp.exp(ALPHA * field)
        shrink = jnp.exp(-BETA * field)
        value = (
            panel(0) * field
            + near_value
            + panel(1) * (grow - shrink)
            + panel(2) * (field - panel(3))
            - source_term[...]
        )
        slope = panel(1) * (ALPHA * grow + BETA * shrink) + panel(2)
        return value, slope

    def apply_precond(value):
        high, low = halves(value)
        left = jnp.concatenate([high, low], axis=1)
        return jnp.stack([both_halves(left[b], precond_w[b]) for b in range(blocks)])

    pl.semaphore_wait(entered_sem.at[0], len(x_peers))
    signal_all(entered_sem.at[1], col_peers)
    field = potential0[...]
    near_now = near_field(0)
    pl.semaphore_wait(entered_sem.at[1], len(col_peers))
    for newton in range(NEWTON):
        turn = 1 + 2 * newton
        value, slope = mismatch(field, near_now)
        p0 = -value
        z0 = apply_precond(p0)
        start_exchange(turn, z0)
        start_beta(newton, p0)
        diagonal = panel(0) + slope
        n0 = near_field(turn, lambda: pass_beta(newton))
        p1 = diagonal * z0 + n0
        z1 = apply_precond(p1)
        start_exchange(turn + 1, z1)
        g00 = finish_beta(newton)
        beta2 = g00 + EPS
        beta = jnp.sqrt(beta2)
        unit = by_column(1.0 / beta)
        v0, p1, direct = p0 * unit, p1 * unit, diagonal * z1 * unit
        parts = [products(v0, p1), products(p1, p1)]
        n1 = near_field(turn + 1)
        p2 = direct + n1 * unit
        parts += [products(v0, p2), products(p1, p2), products(p2, p2)]
        start_sums(newton, parts)
        h00, g11, g02, g12, g22 = finish_sums(newton, 5)
        v00 = g00 / beta2
        pc = h00 - h00 * v00
        pq = g02 - h00 * h00
        cc = jnp.maximum(g11 - h00 * h00 - h00 * pc, 0.0)
        cq = g12 - h00 * g02 - h00 * (g11 - h00 * h00)
        qq = jnp.maximum(g22 - h00 * (2.0 * g12 - h00 * g11), 0.0)
        norm2 = cc + EPS
        gram0 = h00 * h00 + norm2
        over_norm = 1.0 / norm2
        over_gram = 1.0 / gram0
        cross = cq - pq * pc
        ratio = cross * over_norm
        square = (
            qq
            + pq * pq * (v00 - 2.0)
            + ratio * (ratio * cc - 2.0 * cq + 2.0 * pq * pc)
        )
        square = jnp.maximum(square, 0.0) + EPS * norm2
        across = norm2 * pq - h00 * cross
        part = across * over_gram
        y1 = part / (square + part * (across * over_norm))
        y0 = (h00 - (h00 * pq + cross) * y1) * over_gram
        a0 = by_column(y0 - y1 * h00)
        a1 = by_column(y1)
        field = field + (a0 * z0 + a1 * z1)
        near_now = near_now + (a0 * n0 + a1 * n1)
    both_o[0] = field
    both_o[1] = mismatch(field, near_now)[0]

    for turn in range(2 * NEWTON + 1):
        exchange_copy(turn).wait_send()
    for newton in range(NEWTON):
        spread_copy(sums.at[newton], sum_sem.at[newton]).wait_send()
        spread_copy(beta_a.at[newton], beta_sem.at[newton, 0]).wait_send()
        spread_copy(beta_b.at[newton], beta_sem.at[newton, 1]).wait_send()


def body(patches, cols, potential0, source_term, self_coef, nearfield, precond, exch_current, conductance, member, anode_drive, pair_source, pair_count):
    blocks, columns, panels = potential0.shape
    pairs = nearfield.shape[1]
    turns = 2 * NEWTON + 1
    slots = (cols + 2) * blocks
    hbm = pl.BlockSpec(memory_space=pltpu.HBM)
    vmem = pl.BlockSpec(memory_space=pltpu.VMEM)
    out = jax.ShapeDtypeStruct((2, blocks, columns, panels), F32)
    both = pl.pallas_call(
        functools.partial(kernel, patches, cols),
        out_shape=out,
        in_specs=[hbm] * 11,
        out_specs=vmem,
        scratch_shapes=[
            pltpu.SMEM(anode_drive.shape, F32),
            pltpu.SMEM(pair_source.shape, jnp.int32),
            pltpu.SMEM(pair_count.shape, jnp.int32),
            pltpu.VMEM((blocks, columns, panels), F32),
            pltpu.VMEM((blocks, columns, panels), F32),
            pltpu.VMEM((4, blocks, panels), F32),
            pltpu.VMEM((blocks, panels), jnp.int32),
            pltpu.VMEM((blocks, pairs, panels, panels), F32),
            pltpu.VMEM((blocks, pairs * panels, 2 * panels), BF16),
            pltpu.VMEM((blocks, panels, panels), F32),
            pltpu.VMEM((blocks, panels, 2 * panels), BF16),
            pltpu.VMEM((turns, slots, columns, panels), F32),
            pltpu.VMEM((slots, 2 * columns, panels), BF16),
            pltpu.VMEM((NEWTON, patches * cols, 1, 128), F32),
            pltpu.SemaphoreType.DMA((10 + blocks,)),
            pltpu.SemaphoreType.DMA((turns,)),
            pltpu.SemaphoreType.DMA((turns,)),
            pltpu.SemaphoreType.DMA((NEWTON, 2)),
            pltpu.VMEM((NEWTON, patches, 1, 128), F32),
            pltpu.VMEM((NEWTON, cols, 1, 128), F32),
            pltpu.SemaphoreType.DMA((NEWTON, 2, 2)),
            pltpu.SemaphoreType.REGULAR((2,)),
        ],
        compiler_params=pltpu.CompilerParams(
            collective_id=0, has_side_effects=True, vmem_limit_bytes=40 * 1024 * 1024
        ),
        name="newton_gmres",
    )(
        *(
            pltpu.with_memory_space_constraint(array, pltpu.HBM)
            for array in (
                anode_drive,
                pair_source,
                pair_count,
                potential0,
                source_term,
                self_coef,
                nearfield,
                precond,
                exch_current,
                conductance,
                member,
            )
        )
    )
    return both[0], both[1]


def solution(mesh):
    both = ("patch", "col")
    return jax.shard_map(
        functools.partial(body, mesh.shape["patch"], mesh.shape["col"]),
        mesh=mesh,
        in_specs=(
            P(both, None, None),
            P(both, None, None),
            P(both, None),
            P(both, None, None, None),
            P(both, None, None),
            P(both, None),
            P(both, None),
            P(both, None),
            P(),
            P(both, None),
            P(both),
        ),
        out_specs=(P(both, None, None), P(both, None, None)),
        check_vma=False,
    )
```

```python
import functools

import jax
import jax.numpy as jnp
from jax import lax
from jax.experimental import pallas as pl
from jax.experimental.pallas import tpu as pltpu
from jax.sharding import PartitionSpec as P

NEWTON = 2

ALPHA = 0.6
BETA = 0.4
EPS = 1e-06

MESH = pl.DeviceIdType.MESH
F32 = jnp.float32
BF16 = jnp.bfloat16


def halves(array):
    high = array.astype(BF16)
    low = (array - high.astype(F32)).astype(BF16)
    return high, low


def both_halves(left, right):
    rows = left.shape[0] // 2
    wide = jnp.dot(left, right, preferred_element_type=F32)
    half = wide.shape[1] // 2
    return wide[:rows, :half] + (wide[rows:, :half] + wide[:rows, half:]) + wide[rows:, half:]


def kernel(
    patches,
    cols,
    drive_h,
    source_h,
    count_h,
    potential0_h,
    source_term_h,
    self_coef_h,
    nearfield_h,
    precond_h,
    current_h,
    conduct_h,
    member_h,
    both_o,
    drive_s,
    source_s,
    count_s,
    potential0,
    source_term,
    panels,
    member,
    staged,
    weights,
    precond_f,
    precond_w,
    exchange,
    split,
    sums,
    load_sem,
    send_sem,
    recv_sem,
    sum_sem,
    beta_a,
    beta_b,
    beta_sem,
    entered_sem,
):
    patch = lax.axis_index("patch")
    col = lax.axis_index("col")
    blocks, pairs = source_s.shape
    columns = potential0.shape[1]
    slots = exchange.shape[1]

    me = patch * cols + col
    devices = patches * cols

    def peer_col(step):
        return lax.rem(col + step, cols)

    def peer_patch(step):
        return lax.rem(patch + step, patches)

    def everyone():
        def distance(step, size):
            return min(step, size - step)

        steps = [(p, c) for p in range(patches) for c in range(cols) if p or c]
        side = 4
        steps.sort(
            key=lambda s: (
                distance(s[0] // side, patches // side)
                + distance(s[0] % side, side)
                + distance(s[1] // 2, cols // 2)
            ),
            reverse=True,
        )
        near_patch = [peer_patch(p) for p in range(patches)]
        near_col = [peer_col(c) for c in range(cols)]
        return [(near_patch[p], near_col[c]) for p, c in steps]

    others = everyone()
    side = 4
    line, place = patch // side, lax.rem(patch, side)
    col_peers = [{"col": peer_col(step)} for step in range(1, cols)]
    y_peers = [
        {"patch": lax.rem(line + step, patches // side) * side + place}
        for step in range(1, patches // side)
    ]
    x_peers = [{"patch": line * side + lax.rem(place + step, side)} for step in range(1, side)]
    next_peers = [{"patch": peer_patch(1)}, {"patch": peer_patch(patches - 1)}]

    def signal_all(semaphore, targets):
        for target in targets:
            pl.semaphore_signal(semaphore, inc=1, device_id=target, device_id_type=MESH)

    barrier = pltpu.get_barrier_semaphore()
    greeted = x_peers + y_peers + next_peers + col_peers
    signal_all(barrier, greeted)

    loads = [
        pltpu.make_async_copy(potential0_h, potential0, load_sem.at[0]),
        pltpu.make_async_copy(source_term_h, source_term, load_sem.at[1]),
        pltpu.make_async_copy(self_coef_h, panels.at[0], load_sem.at[2]),
        pltpu.make_async_copy(current_h, panels.at[1], load_sem.at[3]),
        pltpu.make_async_copy(conduct_h, panels.at[2], load_sem.at[4]),
        pltpu.make_async_copy(member_h, member, load_sem.at[5]),
        pltpu.make_async_copy(precond_h, precond_f, load_sem.at[6]),
        pltpu.make_async_copy(drive_h, drive_s, load_sem.at[7]),
        pltpu.make_async_copy(source_h, source_s, load_sem.at[8]),
        pltpu.make_async_copy(count_h, count_s, load_sem.at[9]),
    ]
    matrix_loads = [
        pltpu.make_async_copy(nearfield_h.at[b], staged.at[b], load_sem.at[10 + b])
        for b in range(blocks)
    ]
    for load in loads + matrix_loads:
        load.start()

    pl.semaphore_wait(barrier, len(greeted))

    own = pl.ds(pl.multiple_of(col * blocks, blocks), blocks)
    before = pl.ds(cols * blocks, blocks)
    after = pl.ds((cols + 1) * blocks, blocks)
    half = blocks // 2
    core = lax.rem(col, 2)
    chips = cols // 2
    far_chip = lax.rem(col // 2 + chips // 2, chips)
    sibling = {"col": col + 1 - 2 * core}
    near_cols = [lax.rem(col // 2 + step, chips) * 2 for step in (1, chips - 1)]
    near_targets = [{"col": near + side_core} for near in near_cols for side_core in range(2)]
    near_targets.append(sibling)

    def start_exchange(turn, value):
        exchange[turn, own] = value

        def send(kind, source, place, target):
            pltpu.make_async_remote_copy(
                src_ref=exchange.at[turn, source],
                dst_ref=exchange.at[turn, place],
                send_sem=send_sem.at[turn],
                recv_sem=recv_sem.at[turn, kind],
                device_id=target,
                device_id_type=MESH,
            ).start()

        for side_core in range(2):
            piece = pl.ds(col * blocks + side_core * half, half)
            send(1, piece, piece, {"col": far_chip * 2 + side_core})
        for target in near_targets:
            send(0, own, own, target)
        send(0, own, before, next_peers[0])
        send(0, own, after, next_peers[1])

    def exchange_copy(turn, kind, count):
        return pltpu.make_async_remote_copy(
            src_ref=exchange.at[turn, pl.ds(0, count)],
            dst_ref=exchange.at[turn, pl.ds(0, count)],
            send_sem=send_sem.at[turn],
            recv_sem=recv_sem.at[turn, kind],
            device_id=sibling,
            device_id_type=MESH,
        )

    def split_slots(turn, first, count):
        place = pl.ds(first, count)
        high, low = halves(exchange[turn, place])
        split[place, :columns] = high
        split[place, columns:] = low

    def receive(turn):
        exchange_copy(turn, 1, 2 * half).wait_recv()
        for side_core in range(2):
            piece = pl.ds((far_chip * 2 + side_core) * blocks + core * half, half)
            pltpu.make_async_remote_copy(
                src_ref=exchange.at[turn, piece],
                dst_ref=exchange.at[turn, piece],
                send_sem=send_sem.at[turn],
                recv_sem=recv_sem.at[turn, 2],
                device_id=sibling,
                device_id_type=MESH,
            ).start()
        exchange_copy(turn, 0, slots - 3 * blocks).wait_recv()
        group = 2 * blocks
        for step in range(1, chips):
            split_slots(turn, lax.rem(far_chip + step, chips) * group, group)
        split_slots(turn, cols * blocks, group)
        exchange_copy(turn, 2, 2 * half).wait_recv()
        split_slots(turn, far_chip * group, group)

    def near_field(turn, then=lambda: None):
        receive(turn)
        then()

        results = []
        for b in range(blocks):
            left = jnp.concatenate([split[source_s[b, k]] for k in range(pairs)], axis=1)
            results.append(both_halves(left, weights[b]))
        return jnp.stack(results)

    def spread(buffer, mine, semaphores, targets):
        for target in targets:
            pltpu.make_async_remote_copy(
                src_ref=buffer.at[mine],
                dst_ref=buffer.at[mine],
                send_sem=semaphores.at[0],
                recv_sem=semaphores.at[1],
                device_id=target,
                device_id_type=MESH,
            ).start()

    def spread_copy(buffer, semaphores):
        rest = buffer.at[pl.ds(0, buffer.shape[0] - 1)]
        return pltpu.make_async_remote_copy(
            src_ref=rest,
            dst_ref=rest,
            send_sem=semaphores.at[0],
            recv_sem=semaphores.at[1],
            device_id={"col": peer_col(1)},
            device_id_type=MESH,
        )

    patch_peers = [{"patch": peer_patch(step)} for step in range(1, patches)]

    def start_beta(newton, value):
        table = jnp.concatenate(
            [jnp.sum(value * value, axis=0), jnp.zeros((128 - columns, 128), F32)], axis=0
        )
        beta_a[newton, patch] = jnp.sum(table.T, axis=0, keepdims=True)
        spread(beta_a.at[newton], patch, beta_sem.at[newton, 0], patch_peers)

    def pass_beta(newton):
        spread_copy(beta_a.at[newton], beta_sem.at[newton, 0]).wait_recv()
        beta_b[newton, col] = jnp.sum(beta_a[newton], axis=0)
        spread(beta_b.at[newton], col, beta_sem.at[newton, 1], col_peers)

    def finish_beta(newton):
        spread_copy(beta_b.at[newton], beta_sem.at[newton, 1]).wait_recv()
        return jnp.broadcast_to(jnp.sum(beta_b[newton], axis=0), (8, 128))

    def products(left, right):
        return jnp.sum(left * right, axis=0)

    def start_sums(turn, parts):
        rest = jnp.zeros((128 - len(parts) * columns, 128), F32)
        table = jnp.concatenate(parts + [rest], axis=0)
        sums[turn, me] = jnp.sum(table.T, axis=0, keepdims=True)
        spread(sums.at[turn], me, sum_sem.at[turn], others)

    def finish_sums(turn, count):
        spread_copy(sums.at[turn], sum_sem.at[turn]).wait_recv()
        total = jnp.broadcast_to(jnp.sum(sums[turn], axis=0), (8, 128))
        return [
            total if place == 0 else pltpu.roll(total, 128 - place * columns, 1)
            for place in range(count)
        ]

    lane = lax.broadcasted_iota(jnp.int32, (columns, 128), 1)
    row = lax.broadcasted_iota(jnp.int32, (columns, 128), 0)

    def by_column(lanes):
        wide = jnp.broadcast_to(lanes[:1], (columns, 128))
        picked = jnp.sum(jnp.where(lane == row, wide, 0.0), axis=1, keepdims=True)
        return jnp.broadcast_to(picked, (columns, 128))[None]

    loads[0].wait()
    start_exchange(0, potential0[...])
    signal_all(entered_sem.at[0], x_peers)
    for load in loads[1:]:
        load.wait()

    owner = member[...]
    drive = jnp.zeros(owner.shape, F32)
    for place in range(drive_s.shape[0]):
        drive = jnp.where(owner == place, drive_s[place], drive)
    panels[3] = drive
    for b in range(blocks):
        high, low = halves(precond_f[b].T)
        precond_w[b, :, :128] = high
        precond_w[b, :, 128:] = low

    for b in range(blocks):
        matrix_loads[b].wait()

        def prepare(k, carry, b=b):
            live = jnp.where(k < count_s[b], 1.0, 0.0).astype(F32)
            high, low = halves((staged[b, k] * live).T)
            place = pl.ds(pl.multiple_of(k * 128, 128), 128)
            weights[b, place, :128] = high
            weights[b, place, 128:] = low
            return carry

        lax.fori_loop(0, pairs, prepare, 0, unroll=4)

    def panel(place):
        return panels[place][:, None, :]

    def mismatch(field, near_value):
        grow = jnp.exp(ALPHA * field)
        shrink = jnp.exp(-BETA * field)
        value = (
            panel(0) * field
            + near_value
            + panel(1) * (grow - shrink)
            + panel(2) * (field - panel(3))
            - source_term[...]
        )
        slope = panel(1) * (ALPHA * grow + BETA * shrink) + panel(2)
        return value, slope

    def apply_precond(value):
        high, low = halves(value)
        left = jnp.concatenate([high, low], axis=1)
        return jnp.stack([both_halves(left[b], precond_w[b]) for b in range(blocks)])

    pl.semaphore_wait(entered_sem.at[0], len(x_peers))
    signal_all(entered_sem.at[1], col_peers)
    field = potential0[...]
    near_now = near_field(0)
    pl.semaphore_wait(entered_sem.at[1], len(col_peers))
    for newton in range(NEWTON):
        turn = 1 + 2 * newton
        value, slope = mismatch(field, near_now)
        p0 = -value
        z0 = apply_precond(p0)
        start_exchange(turn, z0)
        start_beta(newton, p0)
        diagonal = panel(0) + slope
        n0 = near_field(turn, lambda: pass_beta(newton))
        p1 = diagonal * z0 + n0
        z1 = apply_precond(p1)
        start_exchange(turn + 1, z1)
        g00 = finish_beta(newton)
        beta2 = g00 + EPS
        beta = jnp.sqrt(beta2)
        unit = by_column(1.0 / beta)
        v0, p1, direct = p0 * unit, p1 * unit, diagonal * z1 * unit
        parts = [products(v0, p1), products(p1, p1)]
        n1 = near_field(turn + 1)
        p2 = direct + n1 * unit
        parts += [products(v0, p2), products(p1, p2), products(p2, p2)]
        start_sums(newton, parts)
        h00, g11, g02, g12, g22 = finish_sums(newton, 5)
        v00 = g00 / beta2
        pc = h00 - h00 * v00
        pq = g02 - h00 * h00
        cc = jnp.maximum(g11 - h00 * h00 - h00 * pc, 0.0)
        cq = g12 - h00 * g02 - h00 * (g11 - h00 * h00)
        qq = jnp.maximum(g22 - h00 * (2.0 * g12 - h00 * g11), 0.0)
        norm2 = cc + EPS
        gram0 = h00 * h00 + norm2
        over_norm = 1.0 / norm2
        over_gram = 1.0 / gram0
        cross = cq - pq * pc
        ratio = cross * over_norm
        square = (
            qq
            + pq * pq * (v00 - 2.0)
            + ratio * (ratio * cc - 2.0 * cq + 2.0 * pq * pc)
        )
        square = jnp.maximum(square, 0.0) + EPS * norm2
        across = norm2 * pq - h00 * cross
        part = across * over_gram
        y1 = part / (square + part * (across * over_norm))
        y0 = (h00 - (h00 * pq + cross) * y1) * over_gram
        a0 = by_column(y0 - y1 * h00)
        a1 = by_column(y1)
        field = field + (a0 * z0 + a1 * z1)
        near_now = near_now + (a0 * n0 + a1 * n1)
    both_o[0] = field
    both_o[1] = mismatch(field, near_now)[0]

    for turn in range(2 * NEWTON + 1):
        exchange_copy(turn, 0, slots - blocks).wait_send()
    for newton in range(NEWTON):
        spread_copy(sums.at[newton], sum_sem.at[newton]).wait_send()
        spread_copy(beta_a.at[newton], beta_sem.at[newton, 0]).wait_send()
        spread_copy(beta_b.at[newton], beta_sem.at[newton, 1]).wait_send()


def body(patches, cols, potential0, source_term, self_coef, nearfield, precond, exch_current, conductance, member, anode_drive, pair_source, pair_count):
    blocks, columns, panels = potential0.shape
    pairs = nearfield.shape[1]
    turns = 2 * NEWTON + 1
    slots = (cols + 2) * blocks
    hbm = pl.BlockSpec(memory_space=pltpu.HBM)
    vmem = pl.BlockSpec(memory_space=pltpu.VMEM)
    out = jax.ShapeDtypeStruct((2, blocks, columns, panels), F32)
    both = pl.pallas_call(
        functools.partial(kernel, patches, cols),
        out_shape=out,
        in_specs=[hbm] * 11,
        out_specs=vmem,
        scratch_shapes=[
            pltpu.SMEM(anode_drive.shape, F32),
            pltpu.SMEM(pair_source.shape, jnp.int32),
            pltpu.SMEM(pair_count.shape, jnp.int32),
            pltpu.VMEM((blocks, columns, panels), F32),
            pltpu.VMEM((blocks, columns, panels), F32),
            pltpu.VMEM((4, blocks, panels), F32),
            pltpu.VMEM((blocks, panels), jnp.int32),
            pltpu.VMEM((blocks, pairs, panels, panels), F32),
            pltpu.VMEM((blocks, pairs * panels, 2 * panels), BF16),
            pltpu.VMEM((blocks, panels, panels), F32),
            pltpu.VMEM((blocks, panels, 2 * panels), BF16),
            pltpu.VMEM((turns, slots, columns, panels), F32),
            pltpu.VMEM((slots, 2 * columns, panels), BF16),
            pltpu.VMEM((NEWTON, patches * cols, 1, 128), F32),
            pltpu.SemaphoreType.DMA((10 + blocks,)),
            pltpu.SemaphoreType.DMA((turns,)),
            pltpu.SemaphoreType.DMA((turns, 3)),
            pltpu.SemaphoreType.DMA((NEWTON, 2)),
            pltpu.VMEM((NEWTON, patches, 1, 128), F32),
            pltpu.VMEM((NEWTON, cols, 1, 128), F32),
            pltpu.SemaphoreType.DMA((NEWTON, 2, 2)),
            pltpu.SemaphoreType.REGULAR((2,)),
        ],
        compiler_params=pltpu.CompilerParams(
            collective_id=0, has_side_effects=True, vmem_limit_bytes=40 * 1024 * 1024
        ),
        name="newton_gmres",
    )(
        *(
            pltpu.with_memory_space_constraint(array, pltpu.HBM)
            for array in (
                anode_drive,
                pair_source,
                pair_count,
                potential0,
                source_term,
                self_coef,
                nearfield,
                precond,
                exch_current,
                conductance,
                member,
            )
        )
    )
    return both[0], both[1]


def solution(mesh):
    both = ("patch", "col")
    return jax.shard_map(
        functools.partial(body, mesh.shape["patch"], mesh.shape["col"]),
        mesh=mesh,
        in_specs=(
            P(both, None, None),
            P(both, None, None),
            P(both, None),
            P(both, None, None, None),
            P(both, None, None),
            P(both, None),
            P(both, None),
            P(both, None),
            P(),
            P(both, None),
            P(both),
        ),
        out_specs=(P(both, None, None), P(both, None, None)),
        check_vma=False,
    )
```

```python
import functools

import jax
import jax.numpy as jnp
from jax import lax
from jax.experimental import pallas as pl
from jax.experimental.pallas import tpu as pltpu
from jax.sharding import PartitionSpec as P

NEWTON = 2

ALPHA = 0.6
BETA = 0.4
EPS = 1e-06

MESH = pl.DeviceIdType.MESH
F32 = jnp.float32
BF16 = jnp.bfloat16


def halves(array):
    high = array.astype(BF16)
    low = (array - high.astype(F32)).astype(BF16)
    return high, low


def both_halves(left, right):
    rows = left.shape[0] // 2
    wide = jnp.dot(left, right, preferred_element_type=F32)
    half = wide.shape[1] // 2
    return wide[:rows, :half] + (wide[rows:, :half] + wide[:rows, half:]) + wide[rows:, half:]


def kernel(
    patches,
    cols,
    drive_h,
    source_h,
    count_h,
    potential0_h,
    source_term_h,
    self_coef_h,
    nearfield_h,
    precond_h,
    current_h,
    conduct_h,
    member_h,
    both_o,
    drive_s,
    source_s,
    count_s,
    potential0,
    source_term,
    panels,
    member,
    staged,
    weights,
    precond_f,
    precond_w,
    exchange,
    split,
    sums,
    load_sem,
    send_sem,
    recv_sem,
    sum_sem,
    beta_a,
    beta_b,
    beta_sem,
    entered_sem,
):
    patch = lax.axis_index("patch")
    col = lax.axis_index("col")
    blocks, pairs = source_s.shape
    columns = potential0.shape[1]
    slots = exchange.shape[1]

    me = patch * cols + col
    devices = patches * cols

    def peer_col(step):
        return lax.rem(col + step, cols)

    def peer_patch(step):
        return lax.rem(patch + step, patches)

    def everyone():
        def distance(step, size):
            return min(step, size - step)

        steps = [(p, c) for p in range(patches) for c in range(cols) if p or c]
        side = 4
        steps.sort(
            key=lambda s: (
                distance(s[0] // side, patches // side)
                + distance(s[0] % side, side)
                + distance(s[1] // 2, cols // 2)
            ),
            reverse=True,
        )
        near_patch = [peer_patch(p) for p in range(patches)]
        near_col = [peer_col(c) for c in range(cols)]
        return [(near_patch[p], near_col[c]) for p, c in steps]

    others = everyone()
    side = 4
    line, place = patch // side, lax.rem(patch, side)
    col_peers = [{"col": peer_col(step)} for step in range(1, cols)]
    y_peers = [
        {"patch": lax.rem(line + step, patches // side) * side + place}
        for step in range(1, patches // side)
    ]
    x_peers = [{"patch": line * side + lax.rem(place + step, side)} for step in range(1, side)]
    next_peers = [{"patch": peer_patch(1)}, {"patch": peer_patch(patches - 1)}]

    def signal_all(semaphore, targets):
        for target in targets:
            pl.semaphore_signal(semaphore, inc=1, device_id=target, device_id_type=MESH)

    barrier = pltpu.get_barrier_semaphore()
    greeted = x_peers + y_peers + next_peers + col_peers
    signal_all(barrier, greeted)

    loads = [
        pltpu.make_async_copy(potential0_h, potential0, load_sem.at[0]),
        pltpu.make_async_copy(source_term_h, source_term, load_sem.at[1]),
        pltpu.make_async_copy(self_coef_h, panels.at[0], load_sem.at[2]),
        pltpu.make_async_copy(current_h, panels.at[1], load_sem.at[3]),
        pltpu.make_async_copy(conduct_h, panels.at[2], load_sem.at[4]),
        pltpu.make_async_copy(member_h, member, load_sem.at[5]),
        pltpu.make_async_copy(precond_h, precond_f, load_sem.at[6]),
        pltpu.make_async_copy(drive_h, drive_s, load_sem.at[7]),
        pltpu.make_async_copy(source_h, source_s, load_sem.at[8]),
        pltpu.make_async_copy(count_h, count_s, load_sem.at[9]),
    ]
    matrix_loads = [
        pltpu.make_async_copy(nearfield_h.at[b], staged.at[b], load_sem.at[10 + b])
        for b in range(blocks)
    ]
    for load in loads + matrix_loads:
        load.start()

    pl.semaphore_wait(barrier, len(greeted))

    own = pl.ds(pl.multiple_of(col * blocks, blocks), blocks)
    before = pl.ds(cols * blocks, blocks)
    after = pl.ds((cols + 1) * blocks, blocks)
    half = blocks // 2
    core = lax.rem(col, 2)
    chips = cols // 2
    far_chip = lax.rem(col // 2 + chips // 2, chips)
    sibling = {"col": col + 1 - 2 * core}
    near_cols = [lax.rem(col // 2 + step, chips) * 2 for step in (1, chips - 1)]
    near_targets = [{"col": near + side_core} for near in near_cols for side_core in range(2)]
    near_targets.append(sibling)

    def start_exchange(turn, value):
        exchange[turn, own] = value

        def send(kind, source, place, target):
            pltpu.make_async_remote_copy(
                src_ref=exchange.at[turn, source],
                dst_ref=exchange.at[turn, place],
                send_sem=send_sem.at[turn],
                recv_sem=recv_sem.at[turn, kind],
                device_id=target,
                device_id_type=MESH,
            ).start()

        for side_core in range(2):
            piece = pl.ds(col * blocks + side_core * half, half)
            send(1, piece, piece, {"col": far_chip * 2 + side_core})
        send(0, own, before, next_peers[0])
        send(0, own, after, next_peers[1])
        for target in near_targets:
            send(0, own, own, target)

    def exchange_copy(turn, kind, count):
        return pltpu.make_async_remote_copy(
            src_ref=exchange.at[turn, pl.ds(0, count)],
            dst_ref=exchange.at[turn, pl.ds(0, count)],
            send_sem=send_sem.at[turn],
            recv_sem=recv_sem.at[turn, kind],
            device_id=sibling,
            device_id_type=MESH,
        )

    def split_slots(turn, first, count):
        place = pl.ds(first, count)
        high, low = halves(exchange[turn, place])
        split[place, :columns] = high
        split[place, columns:] = low

    def receive(turn, then):
        exchange_copy(turn, 1, 2 * half).wait_recv()
        for side_core in range(2):
            piece = pl.ds((far_chip * 2 + side_core) * blocks + core * half, half)
            pltpu.make_async_remote_copy(
                src_ref=exchange.at[turn, piece],
                dst_ref=exchange.at[turn, piece],
                send_sem=send_sem.at[turn],
                recv_sem=recv_sem.at[turn, 2],
                device_id=sibling,
                device_id_type=MESH,
            ).start()
        exchange_copy(turn, 0, slots - 3 * blocks).wait_recv()
        group = 2 * blocks
        for step in range(1, chips):
            split_slots(turn, lax.rem(far_chip + step, chips) * group, group)
        split_slots(turn, cols * blocks, group)
        then()
        exchange_copy(turn, 2, 2 * half).wait_recv()
        split_slots(turn, far_chip * group, group)

    def near_field(turn, then=lambda: None):
        receive(turn, then)

        results = []
        for b in range(blocks):
            left = jnp.concatenate([split[source_s[b, k]] for k in range(pairs)], axis=1)
            results.append(both_halves(left, weights[b]))
        return jnp.stack(results)

    def spread(buffer, mine, semaphores, targets):
        for target in targets:
            pltpu.make_async_remote_copy(
                src_ref=buffer.at[mine],
                dst_ref=buffer.at[mine],
                send_sem=semaphores.at[0],
                recv_sem=semaphores.at[1],
                device_id=target,
                device_id_type=MESH,
            ).start()

    def spread_copy(buffer, semaphores):
        rest = buffer.at[pl.ds(0, buffer.shape[0] - 1)]
        return pltpu.make_async_remote_copy(
            src_ref=rest,
            dst_ref=rest,
            send_sem=semaphores.at[0],
            recv_sem=semaphores.at[1],
            device_id={"col": peer_col(1)},
            device_id_type=MESH,
        )

    patch_peers = [{"patch": peer_patch(step)} for step in range(1, patches)]

    def start_beta(newton, value):
        table = jnp.concatenate(
            [jnp.sum(value * value, axis=0), jnp.zeros((128 - columns, 128), F32)], axis=0
        )
        beta_a[newton, patch] = jnp.sum(table.T, axis=0, keepdims=True)
        spread(beta_a.at[newton], patch, beta_sem.at[newton, 0], patch_peers)

    def pass_beta(newton):
        spread_copy(beta_a.at[newton], beta_sem.at[newton, 0]).wait_recv()
        beta_b[newton, col] = jnp.sum(beta_a[newton], axis=0)
        spread(beta_b.at[newton], col, beta_sem.at[newton, 1], col_peers)

    def finish_beta(newton):
        spread_copy(beta_b.at[newton], beta_sem.at[newton, 1]).wait_recv()
        return jnp.broadcast_to(jnp.sum(beta_b[newton], axis=0), (8, 128))

    def products(left, right):
        return jnp.sum(left * right, axis=0)

    def start_sums(turn, parts):
        rest = jnp.zeros((128 - len(parts) * columns, 128), F32)
        table = jnp.concatenate(parts + [rest], axis=0)
        sums[turn, me] = jnp.sum(table.T, axis=0, keepdims=True)
        spread(sums.at[turn], me, sum_sem.at[turn], others)

    def finish_sums(turn, count):
        spread_copy(sums.at[turn], sum_sem.at[turn]).wait_recv()
        total = jnp.broadcast_to(jnp.sum(sums[turn], axis=0), (8, 128))
        return [
            total if place == 0 else pltpu.roll(total, 128 - place * columns, 1)
            for place in range(count)
        ]

    lane = lax.broadcasted_iota(jnp.int32, (columns, 128), 1)
    row = lax.broadcasted_iota(jnp.int32, (columns, 128), 0)

    def by_column(lanes):
        wide = jnp.broadcast_to(lanes[:1], (columns, 128))
        picked = jnp.sum(jnp.where(lane == row, wide, 0.0), axis=1, keepdims=True)
        return jnp.broadcast_to(picked, (columns, 128))[None]

    loads[0].wait()
    start_exchange(0, potential0[...])
    signal_all(entered_sem.at[0], x_peers)
    for load in loads[1:]:
        load.wait()

    owner = member[...]
    drive = jnp.zeros(owner.shape, F32)
    for place in range(drive_s.shape[0]):
        drive = jnp.where(owner == place, drive_s[place], drive)
    panels[3] = drive
    for b in range(blocks):
        high, low = halves(precond_f[b].T)
        precond_w[b, :, :128] = high
        precond_w[b, :, 128:] = low

    for b in range(blocks):
        matrix_loads[b].wait()

        def prepare(k, carry, b=b):
            live = jnp.where(k < count_s[b], 1.0, 0.0).astype(F32)
            high, low = halves((staged[b, k] * live).T)
            place = pl.ds(pl.multiple_of(k * 128, 128), 128)
            weights[b, place, :128] = high
            weights[b, place, 128:] = low
            return carry

        lax.fori_loop(0, pairs, prepare, 0, unroll=4)

    def panel(place):
        return panels[place][:, None, :]

    def mismatch(field, near_value):
        grow = jnp.exp(ALPHA * field)
        shrink = jnp.exp(-BETA * field)
        value = (
            panel(0) * field
            + near_value
            + panel(1) * (grow - shrink)
            + panel(2) * (field - panel(3))
            - source_term[...]
        )
        slope = panel(1) * (ALPHA * grow + BETA * shrink) + panel(2)
        return value, slope

    def apply_precond(value):
        high, low = halves(value)
        left = jnp.concatenate([high, low], axis=1)
        return jnp.stack([both_halves(left[b], precond_w[b]) for b in range(blocks)])

    pl.semaphore_wait(entered_sem.at[0], len(x_peers))
    signal_all(entered_sem.at[1], col_peers)
    field = potential0[...]
    near_now = near_field(0)
    pl.semaphore_wait(entered_sem.at[1], len(col_peers))
    for newton in range(NEWTON):
        turn = 1 + 2 * newton
        value, slope = mismatch(field, near_now)
        p0 = -value
        z0 = apply_precond(p0)
        start_exchange(turn, z0)
        start_beta(newton, p0)
        diagonal = panel(0) + slope
        n0 = near_field(turn, lambda: pass_beta(newton))
        p1 = diagonal * z0 + n0
        z1 = apply_precond(p1)
        start_exchange(turn + 1, z1)
        g00 = finish_beta(newton)
        beta2 = g00 + EPS
        beta = jnp.sqrt(beta2)
        unit = by_column(1.0 / beta)
        v0, p1, direct = p0 * unit, p1 * unit, diagonal * z1 * unit
        parts = [products(v0, p1), products(p1, p1)]
        n1 = near_field(turn + 1)
        p2 = direct + n1 * unit
        parts += [products(v0, p2), products(p1, p2), products(p2, p2)]
        start_sums(newton, parts)
        h00, g11, g02, g12, g22 = finish_sums(newton, 5)
        v00 = g00 / beta2
        pc = h00 - h00 * v00
        pq = g02 - h00 * h00
        cc = jnp.maximum(g11 - h00 * h00 - h00 * pc, 0.0)
        cq = g12 - h00 * g02 - h00 * (g11 - h00 * h00)
        qq = jnp.maximum(g22 - h00 * (2.0 * g12 - h00 * g11), 0.0)
        norm2 = cc + EPS
        gram0 = h00 * h00 + norm2
        over_norm = 1.0 / norm2
        over_gram = 1.0 / gram0
        cross = cq - pq * pc
        ratio = cross * over_norm
        square = (
            qq
            + pq * pq * (v00 - 2.0)
            + ratio * (ratio * cc - 2.0 * cq + 2.0 * pq * pc)
        )
        square = jnp.maximum(square, 0.0) + EPS * norm2
        across = norm2 * pq - h00 * cross
        part = across * over_gram
        y1 = part / (square + part * (across * over_norm))
        y0 = (h00 - (h00 * pq + cross) * y1) * over_gram
        a0 = by_column(y0 - y1 * h00)
        a1 = by_column(y1)
        field = field + (a0 * z0 + a1 * z1)
        near_now = near_now + (a0 * n0 + a1 * n1)
    both_o[0] = field
    both_o[1] = mismatch(field, near_now)[0]

    for turn in range(2 * NEWTON + 1):
        exchange_copy(turn, 0, slots - blocks).wait_send()
    for newton in range(NEWTON):
        spread_copy(sums.at[newton], sum_sem.at[newton]).wait_send()
        spread_copy(beta_a.at[newton], beta_sem.at[newton, 0]).wait_send()
        spread_copy(beta_b.at[newton], beta_sem.at[newton, 1]).wait_send()


def body(patches, cols, potential0, source_term, self_coef, nearfield, precond, exch_current, conductance, member, anode_drive, pair_source, pair_count):
    blocks, columns, panels = potential0.shape
    pairs = nearfield.shape[1]
    turns = 2 * NEWTON + 1
    slots = (cols + 2) * blocks
    hbm = pl.BlockSpec(memory_space=pltpu.HBM)
    vmem = pl.BlockSpec(memory_space=pltpu.VMEM)
    out = jax.ShapeDtypeStruct((2, blocks, columns, panels), F32)
    both = pl.pallas_call(
        functools.partial(kernel, patches, cols),
        out_shape=out,
        in_specs=[hbm] * 11,
        out_specs=vmem,
        scratch_shapes=[
            pltpu.SMEM(anode_drive.shape, F32),
            pltpu.SMEM(pair_source.shape, jnp.int32),
            pltpu.SMEM(pair_count.shape, jnp.int32),
            pltpu.VMEM((blocks, columns, panels), F32),
            pltpu.VMEM((blocks, columns, panels), F32),
            pltpu.VMEM((4, blocks, panels), F32),
            pltpu.VMEM((blocks, panels), jnp.int32),
            pltpu.VMEM((blocks, pairs, panels, panels), F32),
            pltpu.VMEM((blocks, pairs * panels, 2 * panels), BF16),
            pltpu.VMEM((blocks, panels, panels), F32),
            pltpu.VMEM((blocks, panels, 2 * panels), BF16),
            pltpu.VMEM((turns, slots, columns, panels), F32),
            pltpu.VMEM((slots, 2 * columns, panels), BF16),
            pltpu.VMEM((NEWTON, patches * cols, 1, 128), F32),
            pltpu.SemaphoreType.DMA((10 + blocks,)),
            pltpu.SemaphoreType.DMA((turns,)),
            pltpu.SemaphoreType.DMA((turns, 3)),
            pltpu.SemaphoreType.DMA((NEWTON, 2)),
            pltpu.VMEM((NEWTON, patches, 1, 128), F32),
            pltpu.VMEM((NEWTON, cols, 1, 128), F32),
            pltpu.SemaphoreType.DMA((NEWTON, 2, 2)),
            pltpu.SemaphoreType.REGULAR((2,)),
        ],
        compiler_params=pltpu.CompilerParams(
            collective_id=0, has_side_effects=True, vmem_limit_bytes=40 * 1024 * 1024
        ),
        name="newton_gmres",
    )(
        *(
            pltpu.with_memory_space_constraint(array, pltpu.HBM)
            for array in (
                anode_drive,
                pair_source,
                pair_count,
                potential0,
                source_term,
                self_coef,
                nearfield,
                precond,
                exch_current,
                conductance,
                member,
            )
        )
    )
    return both[0], both[1]


def solution(mesh):
    both = ("patch", "col")
    return jax.shard_map(
        functools.partial(body, mesh.shape["patch"], mesh.shape["col"]),
        mesh=mesh,
        in_specs=(
            P(both, None, None),
            P(both, None, None),
            P(both, None),
            P(both, None, None, None),
            P(both, None, None),
            P(both, None),
            P(both, None),
            P(both, None),
            P(),
            P(both, None),
            P(both),
        ),
        out_specs=(P(both, None, None), P(both, None, None)),
        check_vma=False,
    )
```
